256 devices in a mesh: island: 16 (over x, y), row: 4 (over z_hi), col: 4 (over z_lo, core).
Axes of the slice: x: 4, y: 4, z: 8 (z_hi: 4, z_lo: 2; z = z_hi * 2 + z_lo), core: 2. Of those that a mesh axis runs over, the one named last changes fastest.
Arguments:
- weights: float32 [16, 4096, 4096], P('island', 'row', 'col'), may hold values from -6 to 6
- bases: float32 [2, 32, 4096], P(None, None, 'col'), may hold values from -0.09375 to 0.09375
- pairs: int32 [2, 8, 2], replicated, may hold values from 0 to 15, as said below
Outputs:
- updated: float32 [16, 4096, 4096], P('island', 'row', 'col')
The draws below stay inside these ranges and needn't reach their ends.
Inputs may be any that keep to these rules, and one draw needn't show every extreme that they name: In each matching every island appears exactly once among the pairs, so each matching is a perfect matching of the 16 islands.
All inputs are finite; a program needn't handle non-finite values.
Results may differ from the reference program's by a relative error of at most 0.00011.
Values sent between devices are 32-bit elements; how exact they have to be, the bound alone decides.
A program may use at most 64 MiB of HBM per device.

```python
import jax
import jax.numpy as jnp
from jax import lax

D = 4096
RANK = 32
MATCHINGS = 2
COLS = 4096
ISLANDS = 16


def draw_pairs(key, part):
    listing = []
    half = ISLANDS // 2
    for matching in range(MATCHINGS):
        sub = jax.random.fold_in(key, 7 + matching)
        anchor = jax.random.randint(jax.random.fold_in(sub, 1), (), 0, ISLANDS).astype(jnp.int32)
        across = ((anchor + half) % ISLANDS).astype(jnp.int32)
        ranks = jnp.argsort(jax.random.permutation(jax.random.fold_in(sub, 2), ISLANDS)).astype(jnp.int32)
        ranks = ranks.at[anchor].set(-2).at[across].set(-1)
        order = jnp.argsort(ranks, stable=True).astype(jnp.int32)
        paired = order.reshape(half, 2)
        shuffle = jax.random.permutation(jax.random.fold_in(sub, 3), half).astype(jnp.int32)
        paired = paired[shuffle]
        flips = jax.random.randint(jax.random.fold_in(sub, 4), (half,), 0, 2).astype(jnp.int32)
        first = jnp.where(flips == 1, paired[:, 1], paired[:, 0])
        second = jnp.where(flips == 1, paired[:, 0], paired[:, 1])
        listing.append(jnp.stack([first, second], axis=1).astype(jnp.int32))
    return jnp.stack(listing).astype(jnp.int32)


def steps_of(rng, shape, shards, smallest, top_value):
    factor_of, own = 1.0, jax.random.fold_in(rng, 6)
    for position, shards_of in shards:
        steps = jnp.exp(jax.random.uniform(jax.random.fold_in(own, position), (shards_of,), jnp.float32, smallest / len(shards), top_value / len(shards)))
        factor_of = factor_of * jnp.repeat(steps, shape[position] // shards_of).reshape([-1 if axis == position else 1 for axis in range(len(shape))])
    return factor_of


def noise(own_key, shape, deviation, limit, cuts=(), kind=jnp.bfloat16):
    result = jax.random.normal(own_key, shape, jnp.float32) * deviation
    if len(cuts) > 0:
        result = steps_of(own_key, shape, cuts, -0.22, 0.18) * result
    return jnp.clip(result, min=-limit, max=limit).astype(kind)


def setup_inputs(seed: int = 0) -> dict:
    arg_keys = jax.random.split(jax.random.key(seed), 4)
    return {
        "weights": noise(arg_keys[0], (ISLANDS, D, COLS), 1.0, 6.0, ((0, 16), (1, 4), (2, 4)), jnp.float32),
        "bases": noise(arg_keys[1], (MATCHINGS, RANK, COLS), COLS ** -0.5, 0.09375, ((2, 4),), jnp.float32),
        "pairs": draw_pairs(jax.random.fold_in(arg_keys[3], 71), 0),
    }


def partner_list(pair_rows, islands):
    positions = jnp.arange(islands, dtype=jnp.int32)
    first = pair_rows[:, 0].astype(jnp.int32)
    second = pair_rows[:, 1].astype(jnp.int32)
    from_first = jnp.where(first[None, :] == positions[:, None], second[None, :], 0)
    from_second = jnp.where(second[None, :] == positions[:, None], first[None, :], 0)
    return jnp.sum(from_first + from_second, axis=1).astype(jnp.int32)

def orthonormal(left_factor):
    gram_matrix = jnp.dot(left_factor, left_factor.T, precision=lax.Precision.HIGHEST)
    lower_factor = jnp.linalg.cholesky(gram_matrix)
    return jax.scipy.linalg.solve_triangular(lower_factor, left_factor, lower=True)

def reference(weights, bases, pairs):
    current = weights
    for matching in range(MATCHINGS):
        partner_row = partner_list(pairs[matching], ISLANDS)
        left_terms = jnp.einsum('rc,idc->ird', bases[matching], current, precision=lax.Precision.HIGHEST)
        left_factor = left_terms - jnp.take(left_terms, partner_row, axis=0)
        left_basis = jax.vmap(orthonormal)(left_factor)
        right_terms = jnp.einsum('ird,idc->irc', left_basis, current, precision=lax.Precision.HIGHEST)
        right_factor = right_terms + jnp.take(right_terms, partner_row, axis=0)
        current = current - 0.5 * jnp.einsum('ird,irc->idc', left_basis, right_factor, precision=lax.Precision.HIGHEST)
    return current
```

```python
import jax
import jax.numpy as jnp
from jax import lax
from jax.experimental import pallas as pl
from jax.experimental.pallas import tpu as pltpu
from jax.sharding import PartitionSpec as P

MESH = pl.DeviceIdType.MESH
RANK = 32
WIDTH = 1024
TILES = 32
BLOCKS = WIDTH // 128
ISLANDS = 16
SIDE = 4
PEERS = ISLANDS * SIDE
HIGHEST = lax.Precision.HIGHEST


def halves(array):
    high = array.astype(jnp.bfloat16)
    low = (array - high.astype(jnp.float32)).astype(jnp.bfloat16)
    return high, low


def device(island, row, col):
    return {"island": island, "row": row, "col": col}


def exact_dot(left, right, dims):
    return lax.dot_general(
        left, right, (dims, ((), ())), precision=HIGHEST, preferred_element_type=jnp.float32
    )


def inverse(gram):
    rows = lax.broadcasted_iota(jnp.int32, (RANK, RANK), 0)
    cols = lax.broadcasted_iota(jnp.int32, (RANK, RANK), 1)

    def step(pivot, matrix):
        pivot_row = jnp.sum(jnp.where(rows == pivot, matrix, 0.0), axis=0, keepdims=True)
        pivot_col = jnp.sum(jnp.where(cols == pivot, matrix, 0.0), axis=1, keepdims=True)
        corner = jnp.sum(jnp.where(cols[:1] == pivot, pivot_row, 0.0), axis=1, keepdims=True)
        scale = 1.0 / corner
        plain = matrix - (pivot_col * scale) * pivot_row
        in_row, in_col = rows == pivot, cols == pivot
        edge = jnp.where(in_row, pivot_row * scale, pivot_col * scale)
        swept = jnp.where(in_row | in_col, edge, plain)
        return jnp.where(in_row & in_col, -scale, swept)

    return -lax.fori_loop(0, RANK, step, gram)


def exchange_kernel(
    weights_ref, bases_ref, pairs_ref, left_ref, right_ref,
    plain, high_ref, low_ref, partner, sent, arrived, summed, combined, given,
    gram_sent, gram_got, load_sem, send_sem, own_sem, back_sem, get_sem, gram_send, gram_sem,
):
    island, row, col = (lax.axis_index(name) for name in ("island", "row", "col"))
    side, core = col // 2, col % 2
    other = (1 - side) * 2 + core

    loads = []
    for part in range(4):
        rows = pl.ds(part * 256, 256)
        load = pltpu.make_async_copy(
            weights_ref.at[0, rows, :], plain.at[rows, :], load_sem.at[part]
        )
        load.start()
        loads.append(load)

    barrier = pltpu.get_barrier_semaphore()

    def greet(index, carry):
        k, m = index // SIDE, index % SIDE

        @pl.when((k != island) | (m != col))
        def _():
            pl.semaphore_signal(barrier, inc=1, device_id=device(k, row, m), device_id_type=MESH)

        pl.semaphore_signal(barrier, inc=1, device_id=device(k, m, other), device_id_type=MESH)
        return carry

    lax.fori_loop(0, PEERS, greet, 0)
    for step in range(1, SIDE):
        pl.semaphore_signal(
            barrier, inc=1, device_id=device(island, (row + step) % SIDE, col), device_id_type=MESH
        )

    def find(index, carry):
        for matching in range(2):
            found = jnp.int32(0)
            for pair in range(ISLANDS // 2):
                first, second = pairs_ref[matching, pair, 0], pairs_ref[matching, pair, 1]
                found += jnp.where(first == index, second, 0) + jnp.where(second == index, first, 0)
            partner[matching, index] = found
        return carry

    lax.fori_loop(0, ISLANDS, find, 0)

    bases = bases_ref[...].reshape(2 * RANK, WIDTH)
    base_high, base_low = halves(bases)
    base_stack = jnp.concatenate([base_high, base_low], axis=0)
    contract_last = ((1,), (1,))
    contract_first = ((0,), (0,))
    raw_parts = []
    for part in range(4):
        loads[part].wait()
        rows = pl.ds(part * 256, 256)
        high, low = halves(plain[rows, :])
        high_ref[rows, :] = high
        low_ref[rows, :] = low
        wide = lax.dot_general(
            base_stack, high, (contract_last, ((), ())), preferred_element_type=jnp.float32
        )
        fine = lax.dot_general(
            base_high, low, (contract_last, ((), ())), preferred_element_type=jnp.float32
        )
        terms = wide[: 2 * RANK] + (wide[2 * RANK :] + fine)
        for a in range(4):
            for b in range(2):
                sent[0, a * BLOCKS + part * 2 + b] = terms[a * 8 : a * 8 + 8, b * 128 : b * 128 + 128]
        raw_parts.append(terms[RANK:])
    raw_terms = jnp.concatenate(raw_parts, axis=1)

    pl.semaphore_wait(barrier, 2 * PEERS - 1 + SIDE - 1)

    row_owner = core == island % 2
    row_tile = island * 2 + side
    col_owner = row % 2 == (island + core) % 2
    col_tile = island * 2 + row // 2

    def sized(ref, send, recv):
        return pltpu.make_async_remote_copy(
            ref, ref, send, recv, device_id=device(island, row, other), device_id_type=MESH
        )

    def combine(phase, matching, sign):
        for k in range(ISLANDS):
            summed[k] = (arrived[phase, k * 4] + arrived[phase, k * 4 + 1]) + (
                arrived[phase, k * 4 + 2] + arrived[phase, k * 4 + 3]
            )
        for k in range(ISLANDS):
            combined[phase, k] = summed[k] + sign * summed[partner[matching, k]]

    def over_columns(phase, matching):
        def send(tile, carry):
            k = tile // 2
            m = (tile % 2) * 2 + k % 2

            @pl.when((k != island) | (m != col))
            def _():
                pltpu.make_async_remote_copy(
                    sent.at[phase, tile], arrived.at[phase, island * 4 + col],
                    send_sem.at[phase], own_sem.at[phase],
                    device_id=device(k, row, m), device_id_type=MESH,
                ).start()

            return carry

        lax.fori_loop(0, TILES, send, 0)

        @pl.when(row_owner)
        def _():
            arrived[phase, island * 4 + col] = sent[phase, row_tile]
            sized(arrived.at[phase, pl.ds(0, PEERS - 1)], send_sem.at[phase], own_sem.at[phase]).wait_recv()
            combine(phase, matching, -1.0)

            def give(index, carry):
                k, m = index // SIDE, index % SIDE

                @pl.when((k != island) | (m != col))
                def _():
                    pltpu.make_async_remote_copy(
                        combined.at[phase, k], given.at[phase, row_tile],
                        back_sem.at[phase], get_sem.at[phase],
                        device_id=device(k, row, m), device_id_type=MESH,
                    ).start()

                return carry

            lax.fori_loop(0, PEERS, give, 0)
            given[phase, row_tile] = combined[phase, island]
            sized(given.at[phase, pl.ds(0, TILES - 1)], send_sem.at[phase], get_sem.at[phase]).wait_recv()

        @pl.when(jnp.logical_not(row_owner))
        def _():
            sized(given.at[phase], send_sem.at[phase], get_sem.at[phase]).wait_recv()

    def send_over_rows(phase):
        def send(tile, carry):
            k = tile // 2
            m = (tile % 2) * 2 + (k + core) % 2
            pltpu.make_async_remote_copy(
                sent.at[phase, tile], arrived.at[phase, island * 4 + row],
                send_sem.at[phase], own_sem.at[phase],
                device_id=device(k, m, other), device_id_type=MESH,
            ).start()
            return carry

        lax.fori_loop(0, TILES, send, 0)

    def own_over_rows(phase, matching):
        @pl.when(col_owner)
        def _():
            sized(arrived.at[phase], send_sem.at[phase], own_sem.at[phase]).wait_recv()
            combine(phase, matching, 1.0)

            def give(index, carry):
                k, m = index // SIDE, index % SIDE
                pltpu.make_async_remote_copy(
                    combined.at[phase, k], given.at[phase, col_tile],
                    back_sem.at[phase], get_sem.at[phase],
                    device_id=device(k, m, other), device_id_type=MESH,
                ).start()
                return carry

            lax.fori_loop(0, PEERS, give, 0)

    def finish_over_rows(phase):
        sized(given.at[phase], send_sem.at[phase], get_sem.at[phase]).wait_recv()

    def whole(phase):
        return jnp.concatenate(
            [
                jnp.concatenate([given[phase, a * BLOCKS + b] for b in range(BLOCKS)], axis=1)
                for a in range(4)
            ],
            axis=0,
        )

    def put(phase, value, part):
        for a in range(4):
            for b in range(2):
                sent[phase, a * BLOCKS + part * 2 + b] = value[a * 8 : a * 8 + 8, b * 128 : b * 128 + 128]

    def gram_start(matching, factor):
        gram = exact_dot(factor, factor, contract_last)
        gram_sent[matching] = jnp.concatenate([gram, jnp.zeros((RANK, 128 - RANK), jnp.float32)], axis=1)
        gram_got[matching, row] = gram_sent[matching]
        for step in range(1, SIDE):
            pltpu.make_async_remote_copy(
                gram_sent.at[matching], gram_got.at[matching, row],
                gram_send.at[matching], gram_sem.at[matching],
                device_id=device(island, (row + step) % SIDE, col), device_id_type=MESH,
            ).start()

    def gram_finish(matching):
        sized(gram_got.at[matching, pl.ds(0, SIDE - 1)], gram_send.at[matching], gram_sem.at[matching]).wait_recv()
        total = (gram_got[matching, 0] + gram_got[matching, 1]) + (gram_got[matching, 2] + gram_got[matching, 3])
        return inverse(total[:, :RANK])

    lefts, rights = [], []
    for matching in range(2):
        first, second = matching * 2, matching * 2 + 1
        if matching == 1:
            mix = exact_dot(bases_ref[1], rights[0], contract_last)
            terms = raw_terms - exact_dot(mix, lefts[0], ((1,), (0,)))
            for part in range(4):
                put(first, terms[:, part * 256 : part * 256 + 256], part)
        over_columns(first, matching)
        factor = whole(first)
        gram_start(matching, factor)
        factor_high, factor_low = halves(factor)
        factor_stack = jnp.concatenate([factor_high, factor_low], axis=0)
        if matching == 1:
            seen = exact_dot(factor, lefts[0], contract_last)
            drop = exact_dot(seen, rights[0], ((1,), (0,)))
        for part in range(4):
            cols = pl.ds(part * 256, 256)
            wide = jnp.dot(factor_stack, high_ref[:, cols], preferred_element_type=jnp.float32)
            fine = jnp.dot(factor_high, low_ref[:, cols], preferred_element_type=jnp.float32)
            terms = wide[:RANK] + (wide[RANK:] + fine)
            if matching == 1:
                terms = terms - drop[:, part * 256 : part * 256 + 256]
            put(second, terms, part)
        send_over_rows(second)
        left = 0.5 * exact_dot(gram_finish(matching), factor, ((1,), (0,)))
        own_over_rows(second, matching)
        finish_over_rows(second)
        lefts.append(left)
        rights.append(whole(second))
        left_ref[pl.ds(matching * RANK, RANK), :] = left
        right_ref[pl.ds(matching * RANK, RANK), :] = rights[-1]

    for matching in range(2):
        first, second = matching * 2, matching * 2 + 1
        sized(gram_got.at[matching, pl.ds(0, SIDE - 1)], gram_send.at[matching], gram_sem.at[matching]).wait_send()
        sized(sent.at[second], send_sem.at[second], own_sem.at[second]).wait_send()

        @pl.when(row_owner)
        def _():
            sized(sent.at[first, pl.ds(0, TILES - 1)], send_sem.at[first], own_sem.at[first]).wait_send()
            sized(arrived.at[first, pl.ds(0, PEERS - 1)], back_sem.at[first], own_sem.at[first]).wait_send()

        @pl.when(jnp.logical_not(row_owner))
        def _():
            sized(sent.at[first], send_sem.at[first], own_sem.at[first]).wait_send()

        @pl.when(col_owner)
        def _():
            sized(arrived.at[second], back_sem.at[second], own_sem.at[second]).wait_send()


def update_kernel(weights_ref, left_ref, right_ref, out_ref, right_stack):
    @pl.when(pl.program_id(0) == 0)
    def _():
        high, low = halves(right_ref[...])
        right_stack[...] = jnp.concatenate([high, low, high], axis=0)

    high, low = halves(left_ref[...])
    left_stack = jnp.concatenate([high, high, low], axis=0)
    correction = lax.dot_general(
        left_stack, right_stack[...], (((0,), (0,)), ((), ())), preferred_element_type=jnp.float32
    )
    out_ref[0] = weights_ref[0] - correction


def shards(weights, bases, pairs):
    vmem = pl.BlockSpec(memory_space=pltpu.VMEM)
    factors = jax.ShapeDtypeStruct((2 * RANK, WIDTH), jnp.float32)
    left, right = pl.pallas_call(
        exchange_kernel,
        out_shape=(factors, factors),
        in_specs=[pl.BlockSpec(memory_space=pl.ANY), vmem, pl.BlockSpec(memory_space=pltpu.SMEM)],
        out_specs=(vmem, vmem),
        scratch_shapes=[
            pltpu.VMEM((WIDTH, WIDTH), jnp.float32),
            pltpu.VMEM((WIDTH, WIDTH), jnp.bfloat16),
            pltpu.VMEM((WIDTH, WIDTH), jnp.bfloat16),
            pltpu.SMEM((2, ISLANDS), jnp.int32),
            pltpu.VMEM((4, TILES, 8, 128), jnp.float32),
            pltpu.VMEM((4, PEERS, 8, 128), jnp.float32),
            pltpu.VMEM((ISLANDS, 8, 128), jnp.float32),
            pltpu.VMEM((4, ISLANDS, 8, 128), jnp.float32),
            pltpu.VMEM((4, TILES, 8, 128), jnp.float32),
            pltpu.VMEM((2, RANK, 128), jnp.float32),
            pltpu.VMEM((2, SIDE, RANK, 128), jnp.float32),
            pltpu.SemaphoreType.DMA((4,)),
            pltpu.SemaphoreType.DMA((4,)),
            pltpu.SemaphoreType.DMA((4,)),
            pltpu.SemaphoreType.DMA((4,)),
            pltpu.SemaphoreType.DMA((4,)),
            pltpu.SemaphoreType.DMA((2,)),
            pltpu.SemaphoreType.DMA((2,)),
        ],
        compiler_params=pltpu.CompilerParams(
            collective_id=0, has_side_effects=True, vmem_limit_bytes=40 * 2**20
        ),
        name="exchange",
    )(weights, bases, pairs)
    rows = 256
    return pl.pallas_call(
        update_kernel,
        out_shape=jax.ShapeDtypeStruct(weights.shape, jnp.float32),
        grid=(WIDTH // rows,),
        in_specs=[
            pl.BlockSpec((1, rows, WIDTH), lambda i: (0, i, 0)),
            pl.BlockSpec((2 * RANK, rows), lambda i: (0, i)),
            pl.BlockSpec((2 * RANK, WIDTH), lambda i: (0, 0)),
        ],
        out_specs=pl.BlockSpec((1, rows, WIDTH), lambda i: (0, i, 0)),
        scratch_shapes=[pltpu.VMEM((6 * RANK, WIDTH), jnp.bfloat16)],
        name="update",
    )(weights, left, right)


def solution(mesh):
    in_specs = (P("island", "row", "col"), P(None, None, "col"), P())
    out_specs = P("island", "row", "col")
    return jax.shard_map(shards, mesh=mesh, in_specs=in_specs, out_specs=out_specs, check_vma=False)
```

```python
import jax
import jax.numpy as jnp
from jax import lax
from jax.experimental import pallas as pl
from jax.experimental.pallas import tpu as pltpu
from jax.sharding import PartitionSpec as P

MESH = pl.DeviceIdType.MESH
RANK = 32
WIDTH = 1024
TILES = 32
BLOCKS = WIDTH // 128
ISLANDS = 16
SIDE = 4
PEERS = ISLANDS * SIDE
HIGHEST = lax.Precision.HIGHEST
LAST = (((1,), (1,)), ((), ()))
FIRST = (((0,), (0,)), ((), ()))
PLAIN = (((1,), (0,)), ((), ()))


def halves(array):
    high = array.astype(jnp.bfloat16)
    low = (array - high.astype(jnp.float32)).astype(jnp.bfloat16)
    return high, low


def device(island, row, col):
    return {"island": island, "row": row, "col": col}


def exact_dot(left, right, dims):
    return lax.dot_general(left, right, dims, precision=HIGHEST, preferred_element_type=jnp.float32)


def fast_dot(left, right, dims):
    return lax.dot_general(left, right, dims, preferred_element_type=jnp.float32)


def stack(*rows):
    return jnp.concatenate(rows, axis=0)


def eliminate(matrix, double):
    rows = lax.broadcasted_iota(jnp.int32, (RANK, 128), 0)
    lanes = lax.broadcasted_iota(jnp.int32, (1, 128), 1)
    for pivot in range(RANK):
        factor = matrix[:, pivot : pivot + 1]
        here = lanes == pivot
        if double:
            factor = jnp.where(lanes < 64, factor, matrix[:, 64 + pivot : 65 + pivot])
            here = here | (lanes == 64 + pivot)
        else:
            factor = jnp.broadcast_to(factor, (RANK, 128))
        scaled = jnp.where(here, 1.0, matrix[pivot : pivot + 1]) / factor[pivot : pivot + 1]
        rest = jnp.where(here, 0.0, matrix) - factor * scaled
        matrix = jnp.where(rows == pivot, scaled, rest)
    return matrix


def exchange_kernel(
    weights_ref, bases_ref, pairs_ref, left_ref, right_ref,
    plain, high_ref, low_ref, bases_in, partner, sent, arrived, summed,
    near_out, wide_out, late_out, sums_out, last_out, near_in, wide_in, late_in, sums_in, last_in,
    gram_sent, gram_got,
    load_sem, send_sem, own_sem, back_sem, get_sem, gram_send, gram_sem, ready_sem,
):
    island, row, col = (lax.axis_index(name) for name in ("island", "row", "col"))
    side, core = col // 2, col % 2
    other = (1 - side) * 2 + core

    base_load = pltpu.make_async_copy(bases_ref, bases_in, load_sem.at[4])
    base_load.start()
    loads = []
    for part in range(4):
        rows = pl.ds(part * 256, 256)
        load = pltpu.make_async_copy(
            weights_ref.at[0, rows, :], plain.at[rows, :], load_sem.at[part]
        )
        load.start()
        loads.append(load)

    barrier = pltpu.get_barrier_semaphore()

    def greet(index, carry):
        k, m = index // SIDE, index % SIDE

        @pl.when((k != island) | (m != col))
        def _():
            pl.semaphore_signal(barrier, inc=1, device_id=device(k, row, m), device_id_type=MESH)

        return carry

    lax.fori_loop(0, PEERS, greet, 0)
    for step in range(1, SIDE):
        pl.semaphore_signal(
            barrier, inc=1, device_id=device(island, (row + step) % SIDE, col), device_id_type=MESH
        )

    def find(index, carry):
        for matching in range(2):
            found = jnp.int32(0)
            for pair in range(ISLANDS // 2):
                first, second = pairs_ref[matching, 0, pair], pairs_ref[matching, 1, pair]
                found += jnp.where(first == index, second, 0) + jnp.where(second == index, first, 0)
            partner[matching, index] = found
        return carry

    lax.fori_loop(0, ISLANDS, find, 0)

    base_load.wait()
    base_high, base_low = halves(bases_in[...].reshape(2 * RANK, WIDTH))
    base_stack = stack(base_high, base_low)

    def put(flow, value, part):
        for a in range(4):
            for b in range(2):
                sent[flow, a * BLOCKS + part * 2 + b] = value[a * 8 : a * 8 + 8, b * 128 : b * 128 + 128]

    for part in range(4):
        loads[part].wait()
        rows = pl.ds(part * 256, 256)
        high, low = halves(plain[rows, :])
        high_ref[rows, :] = high
        low_ref[rows, :] = low
        wide = fast_dot(base_stack, high, LAST)
        fine = fast_dot(base_high, low, LAST)
        terms = wide[: 2 * RANK] + (wide[2 * RANK :] + fine)
        put(0, terms[:RANK], part)
        put(1, terms[RANK:], part)

    pl.semaphore_wait(barrier, PEERS - 1 + SIDE - 1)
    for step in range(1, SIDE):
        pl.semaphore_signal(
            ready_sem, inc=1, device_id=device(island, (row + step) % SIDE, col), device_id_type=MESH
        )

    row_owner = core == island % 2
    row_tile = island * 2 + side
    col_owner = row % 2 == (island + core) % 2
    col_tile = island * 2 + row // 2

    def sized(ref, send, recv):
        return pltpu.make_async_remote_copy(
            ref, ref, send, recv, device_id=device(island, row, other), device_id_type=MESH
        )

    def add_up(flow, slot):
        for k in range(ISLANDS):
            summed[slot, k] = (arrived[flow, k * 4] + arrived[flow, k * 4 + 1]) + (
                arrived[flow, k * 4 + 2] + arrived[flow, k * 4 + 3]
            )

    def send_over_columns(flow):
        def send(index, carry):
            tile = (index + 2 * island) % TILES
            k = tile // 2
            m = (tile % 2) * 2 + k % 2

            @pl.when((k != island) | (m != col))
            def _():
                pltpu.make_async_remote_copy(
                    sent.at[flow, tile], arrived.at[flow, island * 4 + col],
                    send_sem.at[flow], own_sem.at[flow],
                    device_id=device(k, row, m), device_id_type=MESH,
                ).start()

            return carry

        lax.fori_loop(0, TILES, send, 0)

    def owned_over_columns(flow):
        arrived[flow, island * 4 + col] = sent[flow, row_tile]
        sized(arrived.at[flow, pl.ds(0, PEERS - 1)], send_sem.at[flow], own_sem.at[flow]).wait_recv()
        add_up(flow, flow)

    def give_over_columns(flow, out, into):
        def give(index, carry):
            k, m = (index // SIDE + island) % ISLANDS, index % SIDE

            @pl.when((k != island) | (m != col))
            def _():
                pltpu.make_async_remote_copy(
                    out.at[k], into.at[row_tile], back_sem.at[flow], get_sem.at[flow],
                    device_id=device(k, row, m), device_id_type=MESH,
                ).start()

            return carry

        lax.fori_loop(0, PEERS, give, 0)
        into[row_tile] = out[island]

    def get_over_columns(flow, into):
        @pl.when(row_owner)
        def _():
            sized(into.at[pl.ds(0, TILES - 1)], back_sem.at[flow], get_sem.at[flow]).wait_recv()

        @pl.when(jnp.logical_not(row_owner))
        def _():
            sized(into, back_sem.at[flow], get_sem.at[flow]).wait_recv()

    def send_over_rows(flow):
        def send(index, carry):
            tile = (index + 2 * island) % TILES
            k = tile // 2
            m = (tile % 2) * 2 + (k + core) % 2
            pltpu.make_async_remote_copy(
                sent.at[flow, tile], arrived.at[flow, island * 4 + row],
                send_sem.at[flow], own_sem.at[flow],
                device_id=device(k, m, other), device_id_type=MESH,
            ).start()
            return carry

        lax.fori_loop(0, TILES, send, 0)

    def owned_over_rows(flow):
        sized(arrived.at[flow], send_sem.at[flow], own_sem.at[flow]).wait_recv()
        add_up(flow, flow - 2)

    def give_over_rows(flow, out, into):
        def give(index, carry):
            k, m = (index // SIDE + island) % ISLANDS, index % SIDE
            pltpu.make_async_remote_copy(
                out.at[k], into.at[col_tile], back_sem.at[flow], get_sem.at[flow],
                device_id=device(k, m, other), device_id_type=MESH,
            ).start()
            return carry

        lax.fori_loop(0, PEERS, give, 0)

    def whole(ref, which):
        return stack(
            *(
                jnp.concatenate([ref[a * BLOCKS + b, which] for b in range(BLOCKS)], axis=1)
                for a in range(4)
            )
        )

    def gram_start(slot, gram):
        gram_sent[slot] = gram
        gram_got[slot, row] = gram
        for step in range(1, SIDE):
            pltpu.make_async_remote_copy(
                gram_sent.at[slot], gram_got.at[slot, row], gram_send.at[slot], gram_sem.at[slot],
                device_id=device(island, (row + step) % SIDE, col), device_id_type=MESH,
            ).start()

    def gram_finish(slot):
        sized(gram_got.at[slot, pl.ds(0, SIDE - 1)], gram_send.at[slot], gram_sem.at[slot]).wait_recv()
        return (gram_got[slot, 0] + gram_got[slot, 1]) + (gram_got[slot, 2] + gram_got[slot, 3])

    def times_weights(high, low, count, use):
        both = stack(high, low)
        for part in range(4):
            cols = pl.ds(part * 256, 256)
            wide = fast_dot(both, high_ref[:, cols], PLAIN)
            fine = fast_dot(high, low_ref[:, cols], PLAIN)
            use(wide[:count] + (wide[count:] + fine), part)

    send_over_columns(0)
    send_over_columns(1)

    @pl.when(row_owner)
    def _():
        owned_over_columns(0)
        for k in range(ISLANDS):
            near_out[k, 0] = summed[0, k] - summed[0, partner[0, k]]
        give_over_columns(0, near_out, near_in)
        owned_over_columns(1)
        for k in range(ISLANDS):
            wide_out[k, 0] = near_out[partner[1, k], 0]
            wide_out[k, 1] = summed[1, k] - summed[1, partner[0, k]]
            late_out[k, 0] = summed[1, k] - summed[1, partner[1, k]]
        for k in range(ISLANDS):
            wide_out[k, 2] = wide_out[partner[1, k], 1]
        give_over_columns(1, wide_out, wide_in)
        give_over_columns(2, late_out, late_in)

    get_over_columns(0, near_in)
    near = whole(near_in, 0)
    near_high, near_low = halves(near)
    products = []

    def first_use(value, part):
        put(2, value, part)
        products.append(value)

    times_weights(near_high, near_low, RANK, first_use)
    pl.semaphore_wait(ready_sem, SIDE - 1)
    send_over_rows(2)
    near_product = jnp.concatenate(products, axis=1)

    get_over_columns(1, wide_in)
    far = whole(wide_in, 0)
    far_high, far_low = halves(far)
    near_cross_high, near_cross_low = halves(whole(wide_in, 1))
    far_cross_high, far_cross_low = halves(whole(wide_in, 2))
    lanes = lax.broadcasted_iota(jnp.int32, (RANK, 128), 1)
    block = fast_dot(
        stack(near_high, far_high, near_low, far_low),
        stack(
            near_high, near_cross_high, far_high, far_cross_high,
            near_low, near_cross_low, far_low, far_cross_low,
        ),
        LAST,
    )
    block = block[:64, :128] + (block[:64, 128:] + block[64:, :128])
    gram_start(0, jnp.where(lanes < 64, block[:RANK], block[RANK:]))

    get_over_columns(2, late_in)
    late = whole(late_in, 0)
    late_high, late_low = halves(late)
    later = []
    times_weights(
        stack(late_high, far_high), stack(late_low, far_low), 2 * RANK,
        lambda value, part: later.append(value),
    )
    later = jnp.concatenate(later, axis=1)
    product_high, product_low = halves(stack(near_product, later[RANK:]))

    solved = eliminate(gram_finish(0), True)
    near_inverse, far_inverse = solved[:, :32], solved[:, 64:96]
    mixing = 0.5 * stack(-solved[:, 32:64], solved[:, 96:128])
    mixing_high, mixing_low = halves(mixing)

    def mixed(high, low):
        return fast_dot(mixing_high, high, FIRST) + (
            fast_dot(mixing_high, low, FIRST) + fast_dot(mixing_low, high, FIRST)
        )

    terms = later[:RANK] + mixed(product_high, product_low)
    for part in range(4):
        put(3, terms[:, part * 256 : part * 256 + 256], part)
    send_over_rows(3)

    factor = late + mixed(stack(near_high, far_high), stack(near_low, far_low))
    factor_high, factor_low = halves(factor)
    nothing = jnp.zeros((RANK, WIDTH), jnp.bfloat16)
    block = fast_dot(
        stack(factor_high, factor_low),
        stack(
            factor_high, near_high, far_high, nothing,
            factor_low, near_low, far_low, nothing,
        ),
        LAST,
    )
    gram_start(1, block[:RANK, :128] + (block[:RANK, 128:] + block[RANK:, :128]))

    @pl.when(col_owner)
    def _():
        owned_over_rows(2)
        for k in range(ISLANDS):
            sums_out[k, 0] = summed[0, k] + summed[0, partner[0, k]]
        for k in range(ISLANDS):
            sums_out[k, 1] = sums_out[partner[1, k], 0]
        give_over_rows(3, sums_out, sums_in)

    left_ref[:RANK, :] = 0.5 * exact_dot(near_inverse, near, PLAIN)

    @pl.when(col_owner)
    def _():
        owned_over_rows(3)
        for k in range(ISLANDS):
            last_out[k, 0] = summed[1, k] + summed[1, partner[1, k]]
        give_over_rows(4, last_out, last_in)

    crossed = gram_finish(1)
    left_ref[RANK:, :] = 0.5 * exact_dot(eliminate(crossed, False)[:, :32], factor, PLAIN)
    near_change = -0.5 * exact_dot(crossed[:, 32:64], near_inverse, PLAIN)
    far_change = 0.5 * exact_dot(crossed[:, 64:96], far_inverse, PLAIN)
    sized(sums_in, back_sem.at[3], get_sem.at[3]).wait_recv()
    near_sums = whole(sums_in, 0)
    right_ref[:RANK, :] = near_sums
    change = exact_dot(
        jnp.concatenate([near_change, far_change], axis=1), stack(near_sums, whole(sums_in, 1)), PLAIN
    )
    sized(last_in, back_sem.at[4], get_sem.at[4]).wait_recv()
    right_ref[RANK:, :] = whole(last_in, 0) + change

    for slot in range(2):
        sized(gram_got.at[slot, pl.ds(0, SIDE - 1)], gram_send.at[slot], gram_sem.at[slot]).wait_send()
        sized(sent.at[2 + slot], send_sem.at[2 + slot], own_sem.at[2 + slot]).wait_send()

    @pl.when(row_owner)
    def _():
        for flow in range(2):
            sized(sent.at[flow, pl.ds(0, TILES - 1)], send_sem.at[flow], own_sem.at[flow]).wait_send()
        for flow, count in ((0, 1), (1, 3), (2, 1)):
            sized(
                arrived.at[pl.ds(0, count), pl.ds(0, PEERS - 1)], back_sem.at[flow], get_sem.at[flow]
            ).wait_send()

    @pl.when(jnp.logical_not(row_owner))
    def _():
        for flow in range(2):
            sized(sent.at[flow], send_sem.at[flow], own_sem.at[flow]).wait_send()

    @pl.when(col_owner)
    def _():
        for flow, count in ((3, 2), (4, 1)):
            sized(arrived.at[pl.ds(0, count)], back_sem.at[flow], get_sem.at[flow]).wait_send()


def update_kernel(weights_ref, left_ref, right_ref, out_ref, right_stack):
    rows = out_ref.shape[1]
    step = pl.program_id(0)

    @pl.when(step == 0)
    def _():
        high, low = halves(right_ref[...])
        right_stack[...] = stack(high, low, high)

    high, low = halves(left_ref[:, pl.ds(pl.multiple_of(step * rows, rows), rows)])
    out_ref[0] = weights_ref[0] - fast_dot(stack(high, high, low), right_stack[...], FIRST)


def shards(weights, bases, pairs):
    vmem = pl.BlockSpec(memory_space=pltpu.VMEM)
    anywhere = pl.BlockSpec(memory_space=pl.ANY)
    factors = jax.ShapeDtypeStruct((2 * RANK, WIDTH), jnp.float32)

    def tiles(*lead):
        return pltpu.VMEM((*lead, 8, 128), jnp.float32)

    dma = pltpu.SemaphoreType.DMA
    left, right = pl.pallas_call(
        exchange_kernel,
        out_shape=(factors, factors),
        in_specs=[anywhere, anywhere, pl.BlockSpec(memory_space=pltpu.SMEM)],
        out_specs=(vmem, vmem),
        scratch_shapes=[
            pltpu.VMEM((WIDTH, WIDTH), jnp.float32),
            pltpu.VMEM((WIDTH, WIDTH), jnp.bfloat16),
            pltpu.VMEM((WIDTH, WIDTH), jnp.bfloat16),
            pltpu.VMEM((2, RANK, WIDTH), jnp.float32),
            pltpu.SMEM((2, ISLANDS), jnp.int32),
            tiles(4, TILES),
            tiles(4, PEERS),
            tiles(2, ISLANDS),
            tiles(ISLANDS, 1), tiles(ISLANDS, 3), tiles(ISLANDS, 1), tiles(ISLANDS, 2), tiles(ISLANDS, 1),
            tiles(TILES, 1), tiles(TILES, 3), tiles(TILES, 1), tiles(TILES, 2), tiles(TILES, 1),
            pltpu.VMEM((2, RANK, 128), jnp.float32),
            pltpu.VMEM((2, SIDE, RANK, 128), jnp.float32),
            dma((5,)), dma((4,)), dma((4,)), dma((5,)), dma((5,)), dma((2,)), dma((2,)),
            pltpu.SemaphoreType.REGULAR,
        ],
        compiler_params=pltpu.CompilerParams(
            collective_id=0, has_side_effects=True, vmem_limit_bytes=56 * 2**20
        ),
        name="exchange",
    )(weights, bases, pairs.transpose(0, 2, 1))
    rows = 256
    return pl.pallas_call(
        update_kernel,
        out_shape=jax.ShapeDtypeStruct(weights.shape, jnp.float32),
        grid=(WIDTH // rows,),
        in_specs=[pl.BlockSpec((1, rows, WIDTH), lambda i: (0, i, 0)), vmem, vmem],
        out_specs=pl.BlockSpec((1, rows, WIDTH), lambda i: (0, i, 0)),
        scratch_shapes=[pltpu.VMEM((6 * RANK, WIDTH), jnp.bfloat16)],
        name="update",
    )(weights, left, right)


def solution(mesh):
    in_specs = (P("island", "row", "col"), P(None, None, "col"), P())
    out_specs = P("island", "row", "col")
    return jax.shard_map(shards, mesh=mesh, in_specs=in_specs, out_specs=out_specs, check_vma=False)
```

```python
import jax
import jax.numpy as jnp
from jax import lax
from jax.experimental import pallas as pl
from jax.experimental.pallas import tpu as pltpu
from jax.sharding import PartitionSpec as P

MESH = pl.DeviceIdType.MESH
RANK = 32
WIDTH = 1024
TILES = 32
BLOCKS = WIDTH // 128
ISLANDS = 16
SIDE = 4
PEERS = ISLANDS * SIDE
HIGHEST = lax.Precision.HIGHEST
LAST = (((1,), (1,)), ((), ()))
FIRST = (((0,), (0,)), ((), ()))
PLAIN = (((1,), (0,)), ((), ()))


def halves(array):
    high = array.astype(jnp.bfloat16)
    low = (array - high.astype(jnp.float32)).astype(jnp.bfloat16)
    return high, low


def device(island, row, col):
    return {"island": island, "row": row, "col": col}


def exact_dot(left, right, dims):
    return lax.dot_general(left, right, dims, precision=HIGHEST, preferred_element_type=jnp.float32)


def fast_dot(left, right, dims):
    return lax.dot_general(left, right, dims, preferred_element_type=jnp.float32)


def stack(*rows):
    return jnp.concatenate(rows, axis=0)


def eliminate(matrix, double):
    rows = lax.broadcasted_iota(jnp.int32, (RANK, 128), 0)
    lanes = lax.broadcasted_iota(jnp.int32, (1, 128), 1)
    for pivot in range(RANK):
        factor = matrix[:, pivot : pivot + 1]
        here = lanes == pivot
        if double:
            factor = jnp.where(lanes < 64, factor, matrix[:, 64 + pivot : 65 + pivot])
            here = here | (lanes == 64 + pivot)
        else:
            factor = jnp.broadcast_to(factor, (RANK, 128))
        scaled = jnp.where(here, 1.0, matrix[pivot : pivot + 1]) / factor[pivot : pivot + 1]
        rest = jnp.where(here, 0.0, matrix) - factor * scaled
        matrix = jnp.where(rows == pivot, scaled, rest)
    return matrix


def exchange_kernel(
    weights_ref, bases_ref, pairs_ref, left_ref, right_ref, plain,
    high_ref, low_ref, bases_in, partner, first, arrived_first, sent, arrived, summed,
    pair_out, late_out, sums_out, last_out, pair_in, late_in, sums_in, last_in,
    factors_in, fold_sent, fold_got, gram_sent, gram_got,
    load_sem, send_sem, own_sem, back_sem, get_sem, mate_send, mate_sem, gram_send, gram_sem, ready_sem,
):
    island, row, col = (lax.axis_index(name) for name in ("island", "row", "col"))
    side, core = col // 2, col % 2
    other = (1 - side) * 2 + core
    mate = side * 2 + 1 - core

    barrier = pltpu.get_barrier_semaphore()

    def greet(index, carry):
        k, m = index // SIDE, index % SIDE

        @pl.when((k != island) | (m != col))
        def _():
            pl.semaphore_signal(barrier, inc=1, device_id=device(k, row, m), device_id_type=MESH)

        return carry

    lax.fori_loop(0, PEERS, greet, 0)
    for step in range(1, SIDE):
        pl.semaphore_signal(
            barrier, inc=1, device_id=device(island, (row + step) % SIDE, col), device_id_type=MESH
        )

    base_load = pltpu.make_async_copy(bases_ref, bases_in, load_sem.at[4])
    base_load.start()
    loads = []
    for part in range(4):
        rows = pl.ds(part * 256, 256)
        load = pltpu.make_async_copy(
            weights_ref.at[0, rows, :], plain.at[rows, :], load_sem.at[part]
        )
        load.start()
        loads.append(load)

    def find(index, carry):
        for matching in range(2):
            found = jnp.int32(0)
            for pair in range(ISLANDS // 2):
                first, second = pairs_ref[matching, 0, pair], pairs_ref[matching, 1, pair]
                found += jnp.where(first == index, second, 0) + jnp.where(second == index, first, 0)
            partner[matching, index] = found
        return carry

    lax.fori_loop(0, ISLANDS, find, 0)

    base_load.wait()
    base_high, base_low = halves(bases_in[...].reshape(2 * RANK, WIDTH))
    base_stack = stack(base_high, base_low)

    def put_first(value, part):
        for basis in range(2):
            for a in range(4):
                for b in range(2):
                    first[a * BLOCKS + part * 2 + b, basis] = value[
                        basis * RANK + a * 8 : basis * RANK + a * 8 + 8, b * 128 : b * 128 + 128
                    ]

    def put(flow, value, part):
        for a in range(4):
            for b in range(2):
                sent[flow, a * BLOCKS + part * 2 + b] = value[a * 8 : a * 8 + 8, b * 128 : b * 128 + 128]

    for part in range(4):
        loads[part].wait()
        rows = pl.ds(part * 256, 256)
        high, low = halves(plain[rows, :])
        high_ref[rows, :] = high
        low_ref[rows, :] = low
        wide = fast_dot(base_stack, high, LAST)
        fine = fast_dot(base_high, low, LAST)
        terms = wide[: 2 * RANK] + (wide[2 * RANK :] + fine)
        put_first(terms, part)

    pl.semaphore_wait(barrier, PEERS - 1 + SIDE - 1)
    for step in range(1, SIDE):
        pl.semaphore_signal(
            ready_sem, inc=1, device_id=device(island, (row + step) % SIDE, col), device_id_type=MESH
        )

    row_owner = core == island % 2
    row_tile = island * 2 + side
    col_owner = row % 2 == (island + core) % 2
    col_tile = island * 2 + row // 2

    def sized(ref, send, recv):
        return pltpu.make_async_remote_copy(
            ref, ref, send, recv, device_id=device(island, row, other), device_id_type=MESH
        )

    def add_up(flow):
        for k in range(ISLANDS):
            summed[flow, k] = (arrived[flow, k * 4] + arrived[flow, k * 4 + 1]) + (
                arrived[flow, k * 4 + 2] + arrived[flow, k * 4 + 3]
            )

    def send_over_columns():
        def send(index, carry):
            tile = (index + 2 * island) % TILES
            k = tile // 2
            m = (tile % 2) * 2 + k % 2

            @pl.when((k != island) | (m != col))
            def _():
                pltpu.make_async_remote_copy(
                    first.at[tile], arrived_first.at[island * 4 + col],
                    send_sem.at[0], own_sem.at[0],
                    device_id=device(k, row, m), device_id_type=MESH,
                ).start()

            return carry

        lax.fori_loop(0, TILES, send, 0)

    def give_pairs():
        def give(index, carry):
            k, m = (index // SIDE + island) % ISLANDS, index % SIDE

            @pl.when((k != island) | (m != col))
            def _():
                pltpu.make_async_remote_copy(
                    pair_out.at[m % 2, k], pair_in.at[row_tile], back_sem.at[0], get_sem.at[0],
                    device_id=device(k, row, m), device_id_type=MESH,
                ).start()

            return carry

        lax.fori_loop(0, PEERS, give, 0)
        pair_in[row_tile] = pair_out[core, island]

    def give_late():
        def give(index, carry):
            k = (index // 2 + island) % ISLANDS
            m = (index % 2) * 2 + row_tile // 16

            @pl.when((k != island) | (m != col))
            def _():
                pltpu.make_async_remote_copy(
                    late_out.at[k], late_in.at[row_tile], back_sem.at[1], get_sem.at[1],
                    device_id=device(k, row, m), device_id_type=MESH,
                ).start()

            return carry

        lax.fori_loop(0, 2 * ISLANDS, give, 0)

        @pl.when(row_tile // 16 == core)
        def _():
            late_in[row_tile] = late_out[island]

    def send_over_rows(flow):
        def send(index, carry):
            tile = (index + 2 * island) % TILES
            k = tile // 2
            m = (tile % 2) * 2 + (k + core) % 2
            pltpu.make_async_remote_copy(
                sent.at[flow, tile], arrived.at[flow, island * 4 + row],
                send_sem.at[flow + 1], own_sem.at[flow + 1],
                device_id=device(k, m, other), device_id_type=MESH,
            ).start()
            return carry

        lax.fori_loop(0, TILES, send, 0)

    def owned_over_rows(flow):
        sized(arrived.at[flow], send_sem.at[flow + 1], own_sem.at[flow + 1]).wait_recv()
        add_up(flow)

    def give_over_rows(flow, out, into):
        def give(index, carry):
            k, m = (index // SIDE + island) % ISLANDS, index % SIDE
            pltpu.make_async_remote_copy(
                out.at[k], into.at[col_tile], back_sem.at[flow], get_sem.at[flow],
                device_id=device(k, m, other), device_id_type=MESH,
            ).start()
            return carry

        lax.fori_loop(0, PEERS, give, 0)

    def whole(ref, which):
        return stack(
            *(
                jnp.concatenate([ref[a * BLOCKS + b, which] for b in range(BLOCKS)], axis=1)
                for a in range(4)
            )
        )

    def to_mate(source, target, index):
        copy = pltpu.make_async_remote_copy(
            source, target, mate_send.at[index], mate_sem.at[index],
            device_id=device(island, row, mate), device_id_type=MESH,
        )
        copy.start()
        return copy

    def gram_start(gram):
        gram_sent[...] = gram
        gram_got[row] = gram
        for step in range(1, SIDE):
            pltpu.make_async_remote_copy(
                gram_sent, gram_got.at[row], gram_send.at[1], gram_sem.at[1],
                device_id=device(island, (row + step) % SIDE, col), device_id_type=MESH,
            ).start()

    def gram_finish():
        sized(gram_got.at[pl.ds(0, SIDE - 1)], gram_send.at[1], gram_sem.at[1]).wait_recv()
        return (gram_got[0] + gram_got[1]) + (gram_got[2] + gram_got[3])

    def times_weights(high, low, count, use):
        both = stack(high, low)
        for part in range(4):
            cols = pl.ds(part * 256, 256)
            wide = fast_dot(both, high_ref[:, cols], PLAIN)
            fine = fast_dot(high, low_ref[:, cols], PLAIN)
            use(wide[:count] + (wide[count:] + fine), part)

    send_over_columns()

    @pl.when(row_owner)
    def _():
        arrived_first[island * 4 + col] = first[row_tile]
        sized(arrived_first.at[pl.ds(0, PEERS - 1)], send_sem.at[0], own_sem.at[0]).wait_recv()
        for k in range(ISLANDS):
            for basis in range(2):
                summed[basis, k] = (
                    arrived_first[k * 4, basis] + arrived_first[k * 4 + 1, basis]
                ) + (arrived_first[k * 4 + 2, basis] + arrived_first[k * 4 + 3, basis])
        for k in range(ISLANDS):
            for basis in range(2):
                pair_out[0, k, basis] = summed[basis, k] - summed[basis, partner[0, k]]
        for k in range(ISLANDS):
            pair_out[1, k] = pair_out[0, partner[1, k]]
        give_pairs()
        for k in range(ISLANDS):
            late_out[k, 0] = summed[1, k] - summed[1, partner[1, k]]
        give_late()
        sized(pair_in.at[pl.ds(0, TILES - 1)], back_sem.at[0], get_sem.at[0]).wait_recv()

    @pl.when(jnp.logical_not(row_owner))
    def _():
        sized(pair_in, back_sem.at[0], get_sem.at[0]).wait_recv()

    mine = whole(pair_in, 0)
    factors_in[core] = mine
    mate_copies = [to_mate(factors_in.at[core], factors_in.at[core], 0)]
    mine_high, mine_low = halves(mine)
    cross_high, cross_low = halves(whole(pair_in, 1))
    block = fast_dot(
        stack(mine_high, mine_low),
        stack(mine_high, cross_high, mine_high, cross_high, mine_low, cross_low, mine_low, cross_low),
        LAST,
    )
    block = block[:RANK, :128] + (block[:RANK, 128:] + block[RANK:, :128])
    narrow = lax.broadcasted_iota(jnp.int32, (RANK // 2, 128), 1) < 64
    fold_sent[...] = jnp.where(narrow, block[: RANK // 2], block[RANK // 2 :])
    fold_got[core, row] = fold_sent[...]

    def fold(index, carry):
        m, h = (row + 1 + index // 2) % SIDE, index % 2

        @pl.when((m != row) | (h != core))
        def _():
            pltpu.make_async_remote_copy(
                fold_sent, fold_got.at[core, row], gram_send.at[0], gram_sem.at[0],
                device_id=device(island, m, side * 2 + h), device_id_type=MESH,
            ).start()

        return carry

    lax.fori_loop(0, 2 * SIDE, fold, 0)

    late_share = row_owner & (row_tile // 16 == core)

    @pl.when(late_share)
    def _():
        sized(late_in.at[pl.ds(0, TILES // 2 - 1)], back_sem.at[1], get_sem.at[1]).wait_recv()

    @pl.when(jnp.logical_not(late_share))
    def _():
        sized(late_in.at[pl.ds(0, TILES // 2)], back_sem.at[1], get_sem.at[1]).wait_recv()

    share = late_in.at[pl.ds(core * 16, 16)]
    mate_copies.append(to_mate(share, share, 1))
    for copy in mate_copies:
        copy.wait_recv()
    near, far, late = factors_in[0], factors_in[1], whole(late_in, 0)
    near_high, near_low = halves(near)
    far_high, far_low = halves(far)
    late_high, late_low = halves(late)
    products = []

    def use(value, part):
        put(0, value[:RANK], part)
        products.append(value)

    times_weights(stack(near_high, late_high, far_high), stack(near_low, late_low, far_low), 3 * RANK, use)
    pl.semaphore_wait(ready_sem, SIDE - 1)
    send_over_rows(0)
    products = jnp.concatenate(products, axis=1)
    later = products[RANK:]
    near_product = products[:RANK]
    product_high, product_low = halves(stack(near_product, later[RANK:]))

    sized(arrived_first.at[pl.ds(0, 2 * SIDE - 1)], gram_send.at[0], gram_sem.at[0]).wait_recv()
    near_fold, far_fold = (
        (fold_got[h, 0] + fold_got[h, 1]) + (fold_got[h, 2] + fold_got[h, 3]) for h in range(2)
    )
    solved = eliminate(
        stack(
            jnp.where(narrow, near_fold, pltpu.roll(far_fold, 64, 1)),
            jnp.where(narrow, pltpu.roll(near_fold, 64, 1), far_fold),
        ),
        True,
    )
    near_inverse, far_inverse = solved[:, :32], solved[:, 64:96]
    mixing = 0.5 * stack(-solved[:, 32:64], solved[:, 96:128])
    mixing_high, mixing_low = halves(mixing)

    def mixed(high, low):
        return fast_dot(mixing_high, high, FIRST) + (
            fast_dot(mixing_high, low, FIRST) + fast_dot(mixing_low, high, FIRST)
        )

    terms = later[:RANK] + mixed(product_high, product_low)
    for part in range(4):
        put(1, terms[:, part * 256 : part * 256 + 256], part)
    send_over_rows(1)

    factor = late + mixed(stack(near_high, far_high), stack(near_low, far_low))
    factor_high, factor_low = halves(factor)
    nothing = jnp.zeros((RANK, WIDTH), jnp.bfloat16)
    block = fast_dot(
        stack(factor_high, factor_low),
        stack(
            factor_high, near_high, far_high, nothing,
            factor_low, near_low, far_low, nothing,
        ),
        LAST,
    )
    gram_start(block[:RANK, :128] + (block[:RANK, 128:] + block[RANK:, :128]))

    @pl.when(col_owner)
    def _():
        owned_over_rows(0)
        for k in range(ISLANDS):
            sums_out[k, 0] = summed[0, k] + summed[0, partner[0, k]]
        for k in range(ISLANDS):
            sums_out[k, 1] = sums_out[partner[1, k], 0]
        give_over_rows(2, sums_out, sums_in)

    left_ref[:RANK, :] = 0.5 * exact_dot(near_inverse, near, PLAIN)

    @pl.when(col_owner)
    def _():
        owned_over_rows(1)
        for k in range(ISLANDS):
            last_out[k, 0] = summed[1, k] + summed[1, partner[1, k]]
        give_over_rows(3, last_out, last_in)

    crossed = gram_finish()
    left_ref[RANK:, :] = 0.5 * exact_dot(eliminate(crossed, False)[:, :32], factor, PLAIN)
    near_change = -0.5 * exact_dot(crossed[:, 32:64], near_inverse, PLAIN)
    far_change = 0.5 * exact_dot(crossed[:, 64:96], far_inverse, PLAIN)
    sized(sums_in, back_sem.at[2], get_sem.at[2]).wait_recv()
    near_sums = whole(sums_in, 0)
    right_ref[:RANK, :] = near_sums
    change = exact_dot(
        jnp.concatenate([near_change, far_change], axis=1), stack(near_sums, whole(sums_in, 1)), PLAIN
    )
    sized(last_in, back_sem.at[3], get_sem.at[3]).wait_recv()
    right_ref[RANK:, :] = whole(last_in, 0) + change

    for copy in mate_copies:
        copy.wait_send()
    sized(arrived_first.at[pl.ds(0, 2 * SIDE - 1)], gram_send.at[0], gram_sem.at[0]).wait_send()
    sized(gram_got.at[pl.ds(0, SIDE - 1)], gram_send.at[1], gram_sem.at[1]).wait_send()
    for flow in range(2):
        sized(sent.at[flow], send_sem.at[flow + 1], own_sem.at[flow + 1]).wait_send()

    @pl.when(row_owner)
    def _():
        sized(first.at[pl.ds(0, TILES - 1)], send_sem.at[0], own_sem.at[0]).wait_send()
        sized(arrived_first.at[pl.ds(0, PEERS - 1)], back_sem.at[0], get_sem.at[0]).wait_send()

        @pl.when(late_share)
        def _():
            sized(late_in.at[pl.ds(0, 2 * ISLANDS - 1)], back_sem.at[1], get_sem.at[1]).wait_send()

        @pl.when(jnp.logical_not(late_share))
        def _():
            sized(late_in, back_sem.at[1], get_sem.at[1]).wait_send()

    @pl.when(jnp.logical_not(row_owner))
    def _():
        sized(first, send_sem.at[0], own_sem.at[0]).wait_send()

    @pl.when(col_owner)
    def _():
        for flow, count in ((2, 2), (3, 1)):
            sized(arrived.at[pl.ds(0, count)], back_sem.at[flow], get_sem.at[flow]).wait_send()


def update_kernel(weights_ref, left_ref, right_ref, out_ref, updated, sem):
    parts, rows = updated.shape[:2]
    high, low = halves(right_ref[...])
    right_stack = stack(high, low, high)
    copies = []
    for part in range(parts):
        block = pl.ds(part * rows, rows)
        high, low = halves(left_ref[:, block])
        updated[part] = weights_ref[block, :] - fast_dot(stack(high, high, low), right_stack, FIRST)
        copy = pltpu.make_async_copy(updated.at[part], out_ref.at[0, block, :], sem.at[part])
        copy.start()
        copies.append(copy)
    for copy in copies:
        copy.wait()


def shards(weights, bases, pairs):
    vmem = pl.BlockSpec(memory_space=pltpu.VMEM)
    hbm = pl.BlockSpec(memory_space=pltpu.HBM)
    factors = jax.ShapeDtypeStruct((2 * RANK, WIDTH), jnp.float32)
    tile = jax.ShapeDtypeStruct((WIDTH, WIDTH), jnp.float32)

    def tiles(*lead):
        return pltpu.VMEM((*lead, 8, 128), jnp.float32)

    dma = pltpu.SemaphoreType.DMA
    left, right, plain = pl.pallas_call(
        exchange_kernel,
        out_shape=(factors, factors, tile),
        in_specs=[hbm, hbm, pl.BlockSpec(memory_space=pltpu.SMEM)],
        out_specs=(vmem, vmem, vmem),
        scratch_shapes=[
            pltpu.VMEM((WIDTH, WIDTH), jnp.bfloat16),
            pltpu.VMEM((WIDTH, WIDTH), jnp.bfloat16),
            pltpu.VMEM((2, RANK, WIDTH), jnp.float32),
            pltpu.SMEM((2, ISLANDS), jnp.int32),
            tiles(TILES, 2), tiles(PEERS, 2),
            tiles(2, TILES), tiles(2, PEERS), tiles(2, ISLANDS),
            tiles(2, ISLANDS, 2), tiles(ISLANDS, 1), tiles(ISLANDS, 2), tiles(ISLANDS, 1),
            tiles(TILES, 2), tiles(TILES, 1), tiles(TILES, 2), tiles(TILES, 1),
            pltpu.VMEM((2, RANK, WIDTH), jnp.float32),
            pltpu.VMEM((RANK // 2, 128), jnp.float32),
            pltpu.VMEM((2, SIDE, RANK // 2, 128), jnp.float32),
            pltpu.VMEM((RANK, 128), jnp.float32),
            pltpu.VMEM((SIDE, RANK, 128), jnp.float32),
            dma((5,)), dma((3,)), dma((3,)), dma((4,)), dma((4,)), dma((2,)), dma((2,)), dma((2,)), dma((2,)),
            pltpu.SemaphoreType.REGULAR,
        ],
        compiler_params=pltpu.CompilerParams(
            collective_id=0, has_side_effects=True, vmem_limit_bytes=32 * 2**20
        ),
        name="exchange",
    )(*(pltpu.with_memory_space_constraint(x, pltpu.HBM) for x in (weights, bases, pairs.transpose(0, 2, 1))))
    parts = 8
    return pl.pallas_call(
        update_kernel,
        out_shape=jax.ShapeDtypeStruct(weights.shape, jnp.float32),
        in_specs=[vmem, vmem, vmem],
        out_specs=hbm,
        scratch_shapes=[pltpu.VMEM((parts, WIDTH // parts, WIDTH), jnp.float32), dma((parts,))],
        compiler_params=pltpu.CompilerParams(vmem_limit_bytes=20 * 2**20),
        name="update",
    )(plain, left, right)


def solution(mesh):
    in_specs = (P("island", "row", "col"), P(None, None, "col"), P())
    out_specs = P("island", "row", "col")
    return jax.shard_map(shards, mesh=mesh, in_specs=in_specs, out_specs=out_specs, check_vma=False)
```

```python
import jax
import jax.numpy as jnp
from jax import lax
from jax.experimental import pallas as pl
from jax.experimental.pallas import tpu as pltpu
from jax.sharding import PartitionSpec as P

MESH = pl.DeviceIdType.MESH
RANK = 32
WIDTH = 1024
TILES = 32
BLOCKS = WIDTH // 128
ISLANDS = 16
SIDE = 4
PEERS = ISLANDS * SIDE
BLOCK = 4
HIGHEST = lax.Precision.HIGHEST
LAST = (((1,), (1,)), ((), ()))
FIRST = (((0,), (0,)), ((), ()))
PLAIN = (((1,), (0,)), ((), ()))


def halves(array):
    high = array.astype(jnp.bfloat16)
    low = (array - high.astype(jnp.float32)).astype(jnp.bfloat16)
    return high, low


def device(island, row, col):
    return {"island": island, "row": row, "col": col}


def exact_dot(left, right, dims):
    return lax.dot_general(left, right, dims, precision=HIGHEST, preferred_element_type=jnp.float32)


def fast_dot(left, right, dims):
    return lax.dot_general(left, right, dims, preferred_element_type=jnp.float32)


def stack(*rows):
    return jnp.concatenate(rows, axis=0)


def eliminate(matrix, double):
    rows = lax.broadcasted_iota(jnp.int32, (RANK, 128), 0)
    lanes = lax.broadcasted_iota(jnp.int32, (1, 128), 1)
    position = lanes % 64 if double else lanes
    for start in range(0, RANK, BLOCK):
        pivots = range(start, start + BLOCK)
        factors = []
        for pivot in pivots:
            factor = jnp.broadcast_to(matrix[:, pivot : pivot + 1], (RANK, 128))
            if double:
                second = jnp.broadcast_to(matrix[:, 64 + pivot : 65 + pivot], (RANK, 128))
                factor = jnp.where(lanes < 64, factor, second)
            factors.append(factor)
        here = (position >= start) & (position < start + BLOCK)
        solved = [
            jnp.where(here, jnp.where(position == pivot, 1.0, 0.0), matrix[pivot : pivot + 1])
            for pivot in pivots
        ]
        corner = [[factor[pivot : pivot + 1] for factor in factors] for pivot in pivots]
        for j in range(BLOCK):
            scale = 1.0 / corner[j][j]
            solved[j] = solved[j] * scale
            corner[j] = [entry * scale if m > j else entry for m, entry in enumerate(corner[j])]
            for i in range(j + 1, BLOCK):
                solved[i] = solved[i] - corner[i][j] * solved[j]
                corner[i] = [
                    entry - corner[i][j] * corner[j][m] if m > j else entry
                    for m, entry in enumerate(corner[i])
                ]
        for j in reversed(range(BLOCK)):
            for i in range(j):
                solved[i] = solved[i] - corner[i][j] * solved[j]
        rest = jnp.where(here, 0.0, matrix)
        for factor, row in zip(factors, solved):
            rest = rest - factor * row
        for pivot, row in zip(pivots, solved):
            rest = jnp.where(rows == pivot, row, rest)
        matrix = rest
    return matrix


def exchange_kernel(
    weights_ref, bases_ref, pairs_ref, left_ref, right_ref, plain,
    high_ref, low_ref, bases_in, partner, first, arrived_first, sent, arrived, summed,
    pair_out, late_out, sums_out, last_out, pair_in, late_in, sums_in, last_in,
    factors_in, fold_sent, fold_got, gram_sent, gram_got,
    load_sem, send_sem, own_sem, back_sem, get_sem, mate_send, mate_sem, gram_send, gram_sem, ready_sem,
):
    island, row, col = (lax.axis_index(name) for name in ("island", "row", "col"))
    side, core = col // 2, col % 2
    other = (1 - side) * 2 + core
    mate = side * 2 + 1 - core

    base_load = pltpu.make_async_copy(bases_ref, bases_in, load_sem.at[4])
    base_load.start()
    loads = []
    for part in range(4):
        rows = pl.ds(part * 256, 256)
        load = pltpu.make_async_copy(
            weights_ref.at[0, rows, :], plain.at[rows, :], load_sem.at[part]
        )
        load.start()
        loads.append(load)

    barrier = pltpu.get_barrier_semaphore()
    across, along = island // SIDE, island % SIDE

    def far_first(index):
        return (2 + 3 * index + 3 * (index * (index - 1) // 2)) % SIDE

    def far_island(index):
        return (across + far_first(index // SIDE)) % SIDE * SIDE + (along + far_first(index % SIDE)) % SIDE

    def greet(index, carry):
        k = far_island(index)
        for m in range(SIDE):

            @pl.when((k != island) | (m != col))
            def _():
                pl.semaphore_signal(barrier, inc=1, device_id=device(k, row, m), device_id_type=MESH)

        return carry

    lax.fori_loop(0, ISLANDS, greet, 0)
    for step in range(1, SIDE):
        pl.semaphore_signal(
            barrier, inc=1, device_id=device(island, (row + step) % SIDE, col), device_id_type=MESH
        )

    base_load.wait()
    base_high, base_low = halves(bases_in[...].reshape(2 * RANK, WIDTH))
    base_stack = stack(base_high, base_low)

    def put_first(value, part):
        for basis in range(2):
            for a in range(4):
                for b in range(2):
                    first[a * BLOCKS + part * 2 + b, basis] = value[
                        basis * RANK + a * 8 : basis * RANK + a * 8 + 8, b * 128 : b * 128 + 128
                    ]

    def put(flow, value, part):
        for a in range(4):
            for b in range(2):
                sent[flow, a * BLOCKS + part * 2 + b] = value[a * 8 : a * 8 + 8, b * 128 : b * 128 + 128]

    for part in range(4):
        loads[part].wait()
        rows = pl.ds(part * 256, 256)
        high, low = halves(plain[rows, :])
        high_ref[rows, :] = high
        low_ref[rows, :] = low
        wide = fast_dot(base_stack, high, LAST)
        fine = fast_dot(base_high, low, LAST)
        terms = wide[: 2 * RANK] + (wide[2 * RANK :] + fine)
        put_first(terms, part)

    pl.semaphore_wait(barrier, PEERS - 1 + SIDE - 1)
    for step in range(1, SIDE):
        pl.semaphore_signal(
            ready_sem, inc=1, device_id=device(island, (row + step) % SIDE, col), device_id_type=MESH
        )

    row_owner = core == island % 2
    row_tile = island * 2 + side
    col_owner = row % 2 == (island + core) % 2
    col_tile = island * 2 + row // 2

    def sized(ref, send, recv):
        return pltpu.make_async_remote_copy(
            ref, ref, send, recv, device_id=device(island, row, other), device_id_type=MESH
        )

    def add_up(flow):
        for k in range(ISLANDS):
            summed[flow, k] = (arrived[flow, k * 4] + arrived[flow, k * 4 + 1]) + (
                arrived[flow, k * 4 + 2] + arrived[flow, k * 4 + 3]
            )

    def send_over_columns():
        def send(index, carry):
            k = far_island(index)
            for which in range(2):
                m = which * 2 + k % 2

                @pl.when((k != island) | (m != col))
                def _():
                    pltpu.make_async_remote_copy(
                        first.at[2 * k + which], arrived_first.at[island * 4 + col],
                        send_sem.at[0], own_sem.at[0],
                        device_id=device(k, row, m), device_id_type=MESH,
                    ).start()

            return carry

        lax.fori_loop(0, ISLANDS, send, 0)

    def give_pairs():
        def give(index, carry):
            k = far_island(index)
            for m in range(SIDE):

                @pl.when((k != island) | (m != col))
                def _():
                    pltpu.make_async_remote_copy(
                        pair_out.at[m % 2, k], pair_in.at[row_tile], back_sem.at[0], get_sem.at[0],
                        device_id=device(k, row, m), device_id_type=MESH,
                    ).start()

            return carry

        lax.fori_loop(0, ISLANDS, give, 0)
        pair_in[row_tile] = pair_out[core, island]

    def give_late():
        def give(index, carry):
            k = far_island(index)
            for half in range(2):
                m = half * 2 + row_tile // 16

                @pl.when((k != island) | (m != col))
                def _():
                    pltpu.make_async_remote_copy(
                        late_out.at[k], late_in.at[row_tile], back_sem.at[1], get_sem.at[1],
                        device_id=device(k, row, m), device_id_type=MESH,
                    ).start()

            return carry

        lax.fori_loop(0, ISLANDS, give, 0)

        @pl.when(row_tile // 16 == core)
        def _():
            late_in[row_tile] = late_out[island]

    def send_over_rows(flow):
        def send(index, carry):
            k = far_island(index)
            for which in range(2):
                pltpu.make_async_remote_copy(
                    sent.at[flow, 2 * k + which], arrived.at[flow, island * 4 + row],
                    send_sem.at[flow + 1], own_sem.at[flow + 1],
                    device_id=device(k, which * 2 + (k + core) % 2, other), device_id_type=MESH,
                ).start()
            return carry

        lax.fori_loop(0, ISLANDS, send, 0)

    def owned_over_rows(flow):
        sized(arrived.at[flow], send_sem.at[flow + 1], own_sem.at[flow + 1]).wait_recv()
        add_up(flow)

    def give_over_rows(flow, out, into):
        def give(index, carry):
            k = far_island(index % ISLANDS)
            for near in range(2):
                m = (row + 1 + side + near + 2 * (index // ISLANDS)) % SIDE
                pltpu.make_async_remote_copy(
                    out.at[k], into.at[col_tile], back_sem.at[flow], get_sem.at[flow],
                    device_id=device(k, m, other), device_id_type=MESH,
                ).start()
            return carry

        lax.fori_loop(0, 2 * ISLANDS, give, 0)

    def whole(ref, which):
        return stack(
            *(
                jnp.concatenate([ref[a * BLOCKS + b, which] for b in range(BLOCKS)], axis=1)
                for a in range(4)
            )
        )

    def to_mate(source, target, index):
        copy = pltpu.make_async_remote_copy(
            source, target, mate_send.at[index], mate_sem.at[index],
            device_id=device(island, row, mate), device_id_type=MESH,
        )
        copy.start()
        return copy

    def gram_start(gram):
        gram_sent[...] = gram
        gram_got[row] = gram
        for step in range(1, SIDE):
            pltpu.make_async_remote_copy(
                gram_sent, gram_got.at[row], gram_send.at[1], gram_sem.at[1],
                device_id=device(island, (row + step) % SIDE, col), device_id_type=MESH,
            ).start()

    def gram_finish():
        sized(gram_got.at[pl.ds(0, SIDE - 1)], gram_send.at[1], gram_sem.at[1]).wait_recv()
        return (gram_got[0] + gram_got[1]) + (gram_got[2] + gram_got[3])

    def times_weights(high, low, count, use):
        both = stack(high, low)
        for part in range(4):
            cols = pl.ds(part * 256, 256)
            wide = fast_dot(both, high_ref[:, cols], PLAIN)
            fine = fast_dot(high, low_ref[:, cols], PLAIN)
            use(wide[:count] + (wide[count:] + fine), part)

    send_over_columns()

    def find(index, carry):
        for matching in range(2):
            found = jnp.int32(0)
            for pair in range(ISLANDS // 2):
                first, second = pairs_ref[matching, 0, pair], pairs_ref[matching, 1, pair]
                found += jnp.where(first == index, second, 0) + jnp.where(second == index, first, 0)
            partner[matching, index] = found
        return carry

    lax.fori_loop(0, ISLANDS, find, 0)

    @pl.when(row_owner)
    def _():
        arrived_first[island * 4 + col] = first[row_tile]
        sized(arrived_first.at[pl.ds(0, PEERS - 1)], send_sem.at[0], own_sem.at[0]).wait_recv()
        for k in range(ISLANDS):
            for basis in range(2):
                summed[basis, k] = (
                    arrived_first[k * 4, basis] + arrived_first[k * 4 + 1, basis]
                ) + (arrived_first[k * 4 + 2, basis] + arrived_first[k * 4 + 3, basis])
        for k in range(ISLANDS):
            for basis in range(2):
                pair_out[0, k, basis] = summed[basis, k] - summed[basis, partner[0, k]]
        for k in range(ISLANDS):
            pair_out[1, k] = pair_out[0, partner[1, k]]
        give_pairs()
        for k in range(ISLANDS):
            late_out[k, 0] = summed[1, k] - summed[1, partner[1, k]]
        give_late()
        sized(pair_in.at[pl.ds(0, TILES - 1)], back_sem.at[0], get_sem.at[0]).wait_recv()

    @pl.when(jnp.logical_not(row_owner))
    def _():
        sized(pair_in, back_sem.at[0], get_sem.at[0]).wait_recv()

    mine = whole(pair_in, 0)
    factors_in[core] = mine
    mate_copies = [to_mate(factors_in.at[core], factors_in.at[core], 0)]
    mine_high, mine_low = halves(mine)
    cross_high, cross_low = halves(whole(pair_in, 1))
    block = fast_dot(
        stack(mine_high, mine_low),
        stack(mine_high, cross_high, mine_high, cross_high, mine_low, cross_low, mine_low, cross_low),
        LAST,
    )
    block = block[:RANK, :128] + (block[:RANK, 128:] + block[RANK:, :128])
    narrow = lax.broadcasted_iota(jnp.int32, (RANK // 2, 128), 1) < 64
    fold_sent[...] = jnp.where(narrow, block[: RANK // 2], block[RANK // 2 :])
    fold_got[core, row] = fold_sent[...]

    def fold(index, carry):
        m, h = (row + 1 + index // 2) % SIDE, index % 2

        @pl.when((m != row) | (h != core))
        def _():
            pltpu.make_async_remote_copy(
                fold_sent, fold_got.at[core, row], gram_send.at[0], gram_sem.at[0],
                device_id=device(island, m, side * 2 + h), device_id_type=MESH,
            ).start()

        return carry

    lax.fori_loop(0, 2 * SIDE, fold, 0)

    late_share = row_owner & (row_tile // 16 == core)

    @pl.when(late_share)
    def _():
        sized(late_in.at[pl.ds(0, TILES // 2 - 1)], back_sem.at[1], get_sem.at[1]).wait_recv()

    @pl.when(jnp.logical_not(late_share))
    def _():
        sized(late_in.at[pl.ds(0, TILES // 2)], back_sem.at[1], get_sem.at[1]).wait_recv()

    share = late_in.at[pl.ds(core * 16, 16)]
    mate_copies.append(to_mate(share, share, 1))
    for copy in mate_copies:
        copy.wait_recv()
    near, far, late = factors_in[0], factors_in[1], whole(late_in, 0)
    near_high, near_low = halves(near)
    far_high, far_low = halves(far)
    late_high, late_low = halves(late)
    products = []

    def use(value, part):
        put(0, value[:RANK], part)
        products.append(value)

    times_weights(stack(near_high, late_high, far_high), stack(near_low, late_low, far_low), 3 * RANK, use)
    pl.semaphore_wait(ready_sem, SIDE - 1)
    send_over_rows(0)
    products = jnp.concatenate(products, axis=1)
    later = products[RANK:]
    near_product = products[:RANK]
    product_high, product_low = halves(stack(near_product, later[RANK:]))

    sized(arrived_first.at[pl.ds(0, 2 * SIDE - 1)], gram_send.at[0], gram_sem.at[0]).wait_recv()
    near_fold, far_fold = (
        (fold_got[h, 0] + fold_got[h, 1]) + (fold_got[h, 2] + fold_got[h, 3]) for h in range(2)
    )
    solved = eliminate(
        stack(
            jnp.where(narrow, near_fold, pltpu.roll(far_fold, 64, 1)),
            jnp.where(narrow, pltpu.roll(near_fold, 64, 1), far_fold),
        ),
        True,
    )
    near_inverse, far_inverse = solved[:, :32], solved[:, 64:96]
    mixing = 0.5 * stack(-solved[:, 32:64], solved[:, 96:128])
    mixing_high, mixing_low = halves(mixing)

    def mixed(high, low):
        return fast_dot(mixing_high, high, FIRST) + (
            fast_dot(mixing_high, low, FIRST) + fast_dot(mixing_low, high, FIRST)
        )

    terms = later[:RANK] + mixed(product_high, product_low)
    for part in range(4):
        put(1, terms[:, part * 256 : part * 256 + 256], part)
    send_over_rows(1)

    factor = late + mixed(stack(near_high, far_high), stack(near_low, far_low))
    factor_high, factor_low = halves(factor)
    nothing = jnp.zeros((RANK, WIDTH), jnp.bfloat16)
    block = fast_dot(
        stack(factor_high, factor_low),
        stack(
            factor_high, near_high, far_high, nothing,
            factor_low, near_low, far_low, nothing,
        ),
        LAST,
    )
    gram_start(block[:RANK, :128] + (block[:RANK, 128:] + block[RANK:, :128]))

    @pl.when(col_owner)
    def _():
        owned_over_rows(0)
        for k in range(ISLANDS):
            sums_out[k, 0] = summed[0, k] + summed[0, partner[0, k]]
        for k in range(ISLANDS):
            sums_out[k, 1] = sums_out[partner[1, k], 0]
        give_over_rows(2, sums_out, sums_in)

    left_ref[:RANK, :] = 0.5 * exact_dot(near_inverse, near, PLAIN)

    @pl.when(col_owner)
    def _():
        owned_over_rows(1)
        for k in range(ISLANDS):
            last_out[k, 0] = summed[1, k] + summed[1, partner[1, k]]
        give_over_rows(3, last_out, last_in)

    crossed = gram_finish()
    left_ref[RANK:, :] = 0.5 * exact_dot(eliminate(crossed, False)[:, :32], factor, PLAIN)
    near_change = -0.5 * exact_dot(crossed[:, 32:64], near_inverse, PLAIN)
    far_change = 0.5 * exact_dot(crossed[:, 64:96], far_inverse, PLAIN)
    sized(sums_in, back_sem.at[2], get_sem.at[2]).wait_recv()
    near_sums = whole(sums_in, 0)
    right_ref[:RANK, :] = near_sums
    change = exact_dot(
        jnp.concatenate([near_change, far_change], axis=1), stack(near_sums, whole(sums_in, 1)), PLAIN
    )
    sized(last_in, back_sem.at[3], get_sem.at[3]).wait_recv()
    right_ref[RANK:, :] = whole(last_in, 0) + change

    for copy in mate_copies:
        copy.wait_send()
    sized(arrived_first.at[pl.ds(0, 2 * SIDE - 1)], gram_send.at[0], gram_sem.at[0]).wait_send()
    sized(gram_got.at[pl.ds(0, SIDE - 1)], gram_send.at[1], gram_sem.at[1]).wait_send()
    for flow in range(2):
        sized(sent.at[flow], send_sem.at[flow + 1], own_sem.at[flow + 1]).wait_send()

    @pl.when(row_owner)
    def _():
        sized(first.at[pl.ds(0, TILES - 1)], send_sem.at[0], own_sem.at[0]).wait_send()
        sized(arrived_first.at[pl.ds(0, PEERS - 1)], back_sem.at[0], get_sem.at[0]).wait_send()

        @pl.when(late_share)
        def _():
            sized(late_in.at[pl.ds(0, 2 * ISLANDS - 1)], back_sem.at[1], get_sem.at[1]).wait_send()

        @pl.when(jnp.logical_not(late_share))
        def _():
            sized(late_in, back_sem.at[1], get_sem.at[1]).wait_send()

    @pl.when(jnp.logical_not(row_owner))
    def _():
        sized(first, send_sem.at[0], own_sem.at[0]).wait_send()

    @pl.when(col_owner)
    def _():
        for flow, count in ((2, 2), (3, 1)):
            sized(arrived.at[pl.ds(0, count)], back_sem.at[flow], get_sem.at[flow]).wait_send()


def update_kernel(weights_ref, left_ref, right_ref, out_ref, updated, sem):
    parts, rows = updated.shape[:2]
    high, low = halves(right_ref[...])
    right_stack = stack(high, low, high)
    copies = []
    for part in range(parts):
        block = pl.ds(part * rows, rows)
        high, low = halves(left_ref[:, block])
        updated[part] = weights_ref[block, :] - fast_dot(stack(high, high, low), right_stack, FIRST)
        copy = pltpu.make_async_copy(updated.at[part], out_ref.at[0, block, :], sem.at[part])
        copy.start()
        copies.append(copy)
    for copy in copies:
        copy.wait()


def shards(weights, bases, pairs):
    vmem = pl.BlockSpec(memory_space=pltpu.VMEM)
    hbm = pl.BlockSpec(memory_space=pltpu.HBM)
    factors = jax.ShapeDtypeStruct((2 * RANK, WIDTH), jnp.float32)
    tile = jax.ShapeDtypeStruct((WIDTH, WIDTH), jnp.float32)

    def tiles(*lead):
        return pltpu.VMEM((*lead, 8, 128), jnp.float32)

    dma = pltpu.SemaphoreType.DMA
    left, right, plain = pl.pallas_call(
        exchange_kernel,
        out_shape=(factors, factors, tile),
        in_specs=[hbm, hbm, pl.BlockSpec(memory_space=pltpu.SMEM)],
        out_specs=(vmem, vmem, vmem),
        scratch_shapes=[
            pltpu.VMEM((WIDTH, WIDTH), jnp.bfloat16),
            pltpu.VMEM((WIDTH, WIDTH), jnp.bfloat16),
            pltpu.VMEM((2, RANK, WIDTH), jnp.float32),
            pltpu.SMEM((2, ISLANDS), jnp.int32),
            tiles(TILES, 2), tiles(PEERS, 2),
            tiles(2, TILES), tiles(2, PEERS), tiles(2, ISLANDS),
            tiles(2, ISLANDS, 2), tiles(ISLANDS, 1), tiles(ISLANDS, 2), tiles(ISLANDS, 1),
            tiles(TILES, 2), tiles(TILES, 1), tiles(TILES, 2), tiles(TILES, 1),
            pltpu.VMEM((2, RANK, WIDTH), jnp.float32),
            pltpu.VMEM((RANK // 2, 128), jnp.float32),
            pltpu.VMEM((2, SIDE, RANK // 2, 128), jnp.float32),
            pltpu.VMEM((RANK, 128), jnp.float32),
            pltpu.VMEM((SIDE, RANK, 128), jnp.float32),
            dma((5,)), dma((3,)), dma((3,)), dma((4,)), dma((4,)), dma((2,)), dma((2,)), dma((2,)), dma((2,)),
            pltpu.SemaphoreType.REGULAR,
        ],
        compiler_params=pltpu.CompilerParams(
            collective_id=0, has_side_effects=True, vmem_limit_bytes=32 * 2**20
        ),
        name="exchange",
    )(*(pltpu.with_memory_space_constraint(x, pltpu.HBM) for x in (weights, bases, pairs.transpose(0, 2, 1))))
    parts = 8
    return pl.pallas_call(
        update_kernel,
        out_shape=jax.ShapeDtypeStruct(weights.shape, jnp.float32),
        in_specs=[vmem, vmem, vmem],
        out_specs=hbm,
        scratch_shapes=[pltpu.VMEM((parts, WIDTH // parts, WIDTH), jnp.float32), dma((parts,))],
        compiler_params=pltpu.CompilerParams(vmem_limit_bytes=20 * 2**20),
        name="update",
    )(plain, left, right)


def solution(mesh):
    in_specs = (P("island", "row", "col"), P(None, None, "col"), P())
    out_specs = P("island", "row", "col")
    return jax.shard_map(shards, mesh=mesh, in_specs=in_specs, out_specs=out_specs, check_vma=False)
```

```python
import jax
import jax.numpy as jnp
from jax import lax
from jax.experimental import pallas as pl
from jax.experimental.pallas import tpu as pltpu
from jax.sharding import PartitionSpec as P

MESH = pl.DeviceIdType.MESH
RANK = 32
WIDTH = 1024
TILES = 32
BLOCKS = WIDTH // 128
ISLANDS = 16
SIDE = 4
PEERS = ISLANDS * SIDE
BLOCK = 4
HIGHEST = lax.Precision.HIGHEST
LAST = (((1,), (1,)), ((), ()))
FIRST = (((0,), (0,)), ((), ()))
PLAIN = (((1,), (0,)), ((), ()))


def halves(array):
    high = array.astype(jnp.bfloat16)
    low = (array - high.astype(jnp.float32)).astype(jnp.bfloat16)
    return high, low


def device(island, row, col):
    return {"island": island, "row": row, "col": col}


def exact_dot(left, right, dims):
    return lax.dot_general(left, right, dims, precision=HIGHEST, preferred_element_type=jnp.float32)


def fast_dot(left, right, dims):
    return lax.dot_general(left, right, dims, preferred_element_type=jnp.float32)


def stack(*rows):
    return jnp.concatenate(rows, axis=0)


def eliminate(matrix, double):
    rows = lax.broadcasted_iota(jnp.int32, (RANK, 128), 0)
    lanes = lax.broadcasted_iota(jnp.int32, (1, 128), 1)
    position = lanes % 64 if double else lanes
    for start in range(0, RANK, BLOCK):
        pivots = range(start, start + BLOCK)
        factors = []
        for pivot in pivots:
            factor = jnp.broadcast_to(matrix[:, pivot : pivot + 1], (RANK, 128))
            if double:
                second = jnp.broadcast_to(matrix[:, 64 + pivot : 65 + pivot], (RANK, 128))
                factor = jnp.where(lanes < 64, factor, second)
            factors.append(factor)
        here = (position >= start) & (position < start + BLOCK)
        solved = [
            jnp.where(here, jnp.where(position == pivot, 1.0, 0.0), matrix[pivot : pivot + 1])
            for pivot in pivots
        ]
        corner = [[factor[pivot : pivot + 1] for factor in factors] for pivot in pivots]
        for j in range(BLOCK):
            scale = 1.0 / corner[j][j]
            solved[j] = solved[j] * scale
            corner[j] = [entry * scale if m > j else entry for m, entry in enumerate(corner[j])]
            for i in range(j + 1, BLOCK):
                solved[i] = solved[i] - corner[i][j] * solved[j]
                corner[i] = [
                    entry - corner[i][j] * corner[j][m] if m > j else entry
                    for m, entry in enumerate(corner[i])
                ]
        for j in reversed(range(BLOCK)):
            for i in range(j):
                solved[i] = solved[i] - corner[i][j] * solved[j]
        rest = jnp.where(here, 0.0, matrix)
        for factor, row in zip(factors, solved):
            rest = rest - factor * row
        for pivot, row in zip(pivots, solved):
            rest = jnp.where(rows == pivot, row, rest)
        matrix = rest
    return matrix


def exchange_kernel(
    weights_ref, bases_ref, pairs_ref, left_ref, right_ref, plain,
    high_ref, low_ref, bases_in, partner, first, arrived_first, sent, arrived, summed,
    pair_out, late_out, sums_out, last_out, pair_in, late_in, sums_in, last_in,
    factors_in, fold_sent, fold_got, gram_sent, gram_got,
    load_sem, send_sem, own_sem, back_sem, get_sem, mate_send, mate_sem, gram_send, gram_sem, ready_sem,
):
    island, row, col = (lax.axis_index(name) for name in ("island", "row", "col"))
    side, core = col // 2, col % 2
    other = (1 - side) * 2 + core
    mate = side * 2 + 1 - core

    base_load = pltpu.make_async_copy(bases_ref, bases_in, load_sem.at[4])
    base_load.start()
    loads = []
    for part in range(4):
        rows = pl.ds(part * 256, 256)
        load = pltpu.make_async_copy(
            weights_ref.at[0, rows, :], plain.at[rows, :], load_sem.at[part]
        )
        load.start()
        loads.append(load)

    barrier = pltpu.get_barrier_semaphore()
    across, along = island // SIDE, island % SIDE

    def far_first(index):
        return (2 + 3 * index + 3 * (index * (index - 1) // 2)) % SIDE

    def far_island(index):
        return (across + far_first(index // SIDE)) % SIDE * SIDE + (along + far_first(index % SIDE)) % SIDE

    def greet(index, carry):
        k = far_island(index)
        for m in range(SIDE):

            @pl.when((k != island) | (m != col))
            def _():
                pl.semaphore_signal(barrier, inc=1, device_id=device(k, row, m), device_id_type=MESH)

        return carry

    lax.fori_loop(0, ISLANDS, greet, 0, unroll=True)
    for step in range(1, SIDE):
        pl.semaphore_signal(
            barrier, inc=1, device_id=device(island, (row + step) % SIDE, col), device_id_type=MESH
        )

    base_load.wait()
    base_high, base_low = halves(bases_in[...].reshape(2 * RANK, WIDTH))
    base_stack = stack(base_high, base_low)

    def put_first(value, part):
        for basis in range(2):
            for a in range(4):
                for b in range(2):
                    first[a * BLOCKS + part * 2 + b, basis] = value[
                        basis * RANK + a * 8 : basis * RANK + a * 8 + 8, b * 128 : b * 128 + 128
                    ]

    def put(flow, value, part):
        for a in range(4):
            for b in range(2):
                sent[flow, a * BLOCKS + part * 2 + b] = value[a * 8 : a * 8 + 8, b * 128 : b * 128 + 128]

    for part in range(4):
        loads[part].wait()
        rows = pl.ds(part * 256, 256)
        high, low = halves(plain[rows, :])
        high_ref[rows, :] = high
        low_ref[rows, :] = low
        wide = fast_dot(base_stack, high, LAST)
        fine = fast_dot(base_high, low, LAST)
        terms = wide[: 2 * RANK] + (wide[2 * RANK :] + fine)
        put_first(terms, part)

    pl.semaphore_wait(barrier, PEERS - 1 + SIDE - 1)
    for step in range(1, SIDE):
        pl.semaphore_signal(
            ready_sem, inc=1, device_id=device(island, (row + step) % SIDE, col), device_id_type=MESH
        )

    row_owner = core == island % 2
    row_tile = island * 2 + side
    col_owner = row % 2 == (island + core) % 2
    col_tile = island * 2 + row // 2

    def sized(ref, send, recv):
        return pltpu.make_async_remote_copy(
            ref, ref, send, recv, device_id=device(island, row, other), device_id_type=MESH
        )

    def add_up(flow):
        for k in range(ISLANDS):
            summed[flow, k] = (arrived[flow, k * 4] + arrived[flow, k * 4 + 1]) + (
                arrived[flow, k * 4 + 2] + arrived[flow, k * 4 + 3]
            )

    def send_over_columns():
        def send(index, carry):
            k = far_island(index)
            for which in range(2):
                m = which * 2 + k % 2

                @pl.when((k != island) | (m != col))
                def _():
                    pltpu.make_async_remote_copy(
                        first.at[2 * k + which], arrived_first.at[island * 4 + col],
                        send_sem.at[0], own_sem.at[0],
                        device_id=device(k, row, m), device_id_type=MESH,
                    ).start()

            return carry

        lax.fori_loop(0, ISLANDS, send, 0, unroll=True)

    def give_pairs():
        def give(index, carry):
            k = far_island(index)
            for m in range(SIDE):

                @pl.when((k != island) | (m != col))
                def _():
                    pltpu.make_async_remote_copy(
                        pair_out.at[m % 2, k], pair_in.at[row_tile], back_sem.at[0], get_sem.at[0],
                        device_id=device(k, row, m), device_id_type=MESH,
                    ).start()

            return carry

        lax.fori_loop(0, ISLANDS, give, 0, unroll=True)
        pair_in[row_tile] = pair_out[core, island]

    def give_late():
        def give(index, carry):
            k = far_island(index)
            for half in range(2):
                m = half * 2 + row_tile // 16

                @pl.when((k != island) | (m != col))
                def _():
                    pltpu.make_async_remote_copy(
                        late_out.at[k], late_in.at[row_tile], back_sem.at[1], get_sem.at[1],
                        device_id=device(k, row, m), device_id_type=MESH,
                    ).start()

            return carry

        lax.fori_loop(0, ISLANDS, give, 0, unroll=True)

        @pl.when(row_tile // 16 == core)
        def _():
            late_in[row_tile] = late_out[island]

    def send_over_rows(flow):
        def send(index, carry):
            k = far_island(index)
            for which in range(2):
                pltpu.make_async_remote_copy(
                    sent.at[flow, 2 * k + which], arrived.at[flow, island * 4 + row],
                    send_sem.at[flow + 1], own_sem.at[flow + 1],
                    device_id=device(k, which * 2 + (k + core) % 2, other), device_id_type=MESH,
                ).start()
            return carry

        lax.fori_loop(0, ISLANDS, send, 0, unroll=True)

    def owned_over_rows(flow):
        sized(arrived.at[flow], send_sem.at[flow + 1], own_sem.at[flow + 1]).wait_recv()
        add_up(flow)

    def give_over_rows(flow, out, into):
        def give(index, carry):
            k = far_island(index % ISLANDS)
            for near in range(2):
                m = (row + 1 + side + near + 2 * (index // ISLANDS)) % SIDE
                pltpu.make_async_remote_copy(
                    out.at[k], into.at[col_tile], back_sem.at[flow], get_sem.at[flow],
                    device_id=device(k, m, other), device_id_type=MESH,
                ).start()
            return carry

        lax.fori_loop(0, 2 * ISLANDS, give, 0, unroll=True)

    def whole(ref, which):
        return stack(
            *(
                jnp.concatenate([ref[a * BLOCKS + b, which] for b in range(BLOCKS)], axis=1)
                for a in range(4)
            )
        )

    def to_mate(source, target, index):
        copy = pltpu.make_async_remote_copy(
            source, target, mate_send.at[index], mate_sem.at[index],
            device_id=device(island, row, mate), device_id_type=MESH,
        )
        copy.start()
        return copy

    def gram_start(gram):
        gram_sent[...] = gram
        gram_got[row] = gram
        for step in range(1, SIDE):
            pltpu.make_async_remote_copy(
                gram_sent, gram_got.at[row], gram_send.at[1], gram_sem.at[1],
                device_id=device(island, (row + step) % SIDE, col), device_id_type=MESH,
            ).start()

    def gram_finish():
        sized(gram_got.at[pl.ds(0, SIDE - 1)], gram_send.at[1], gram_sem.at[1]).wait_recv()
        return (gram_got[0] + gram_got[1]) + (gram_got[2] + gram_got[3])

    def times_weights(high, low, count, use):
        both = stack(high, low)
        for part in range(4):
            cols = pl.ds(part * 256, 256)
            wide = fast_dot(both, high_ref[:, cols], PLAIN)
            fine = fast_dot(high, low_ref[:, cols], PLAIN)
            use(wide[:count] + (wide[count:] + fine), part)

    send_over_columns()

    def find(index, carry):
        for matching in range(2):
            found = jnp.int32(0)
            for pair in range(ISLANDS // 2):
                first, second = pairs_ref[matching, 0, pair], pairs_ref[matching, 1, pair]
                found += jnp.where(first == index, second, 0) + jnp.where(second == index, first, 0)
            partner[matching, index] = found
        return carry

    lax.fori_loop(0, ISLANDS, find, 0)

    @pl.when(row_owner)
    def _():
        arrived_first[island * 4 + col] = first[row_tile]
        sized(arrived_first.at[pl.ds(0, PEERS - 1)], send_sem.at[0], own_sem.at[0]).wait_recv()
        for k in range(ISLANDS):
            for basis in range(2):
                summed[basis, k] = (
                    arrived_first[k * 4, basis] + arrived_first[k * 4 + 1, basis]
                ) + (arrived_first[k * 4 + 2, basis] + arrived_first[k * 4 + 3, basis])
        for k in range(ISLANDS):
            for basis in range(2):
                pair_out[0, k, basis] = summed[basis, k] - summed[basis, partner[0, k]]
        for k in range(ISLANDS):
            pair_out[1, k] = pair_out[0, partner[1, k]]
        give_pairs()
        for k in range(ISLANDS):
            late_out[k, 0] = summed[1, k] - summed[1, partner[1, k]]
        give_late()
        sized(pair_in.at[pl.ds(0, TILES - 1)], back_sem.at[0], get_sem.at[0]).wait_recv()

    @pl.when(jnp.logical_not(row_owner))
    def _():
        sized(pair_in, back_sem.at[0], get_sem.at[0]).wait_recv()

    mine = whole(pair_in, 0)
    factors_in[core] = mine
    mate_copies = [to_mate(factors_in.at[core], factors_in.at[core], 0)]
    mine_high, mine_low = halves(mine)
    cross_high, cross_low = halves(whole(pair_in, 1))
    block = fast_dot(
        stack(mine_high, mine_low),
        stack(mine_high, cross_high, mine_high, cross_high, mine_low, cross_low, mine_low, cross_low),
        LAST,
    )
    block = block[:RANK, :128] + (block[:RANK, 128:] + block[RANK:, :128])
    narrow = lax.broadcasted_iota(jnp.int32, (RANK // 2, 128), 1) < 64
    fold_sent[...] = jnp.where(narrow, block[: RANK // 2], block[RANK // 2 :])
    fold_got[core, row] = fold_sent[...]

    def fold(index, carry):
        m, h = (row + 1 + index // 2) % SIDE, index % 2

        @pl.when((m != row) | (h != core))
        def _():
            pltpu.make_async_remote_copy(
                fold_sent, fold_got.at[core, row], gram_send.at[0], gram_sem.at[0],
                device_id=device(island, m, side * 2 + h), device_id_type=MESH,
            ).start()

        return carry

    lax.fori_loop(0, 2 * SIDE, fold, 0)

    late_share = row_owner & (row_tile // 16 == core)

    @pl.when(late_share)
    def _():
        sized(late_in.at[pl.ds(0, TILES // 2 - 1)], back_sem.at[1], get_sem.at[1]).wait_recv()

    @pl.when(jnp.logical_not(late_share))
    def _():
        sized(late_in.at[pl.ds(0, TILES // 2)], back_sem.at[1], get_sem.at[1]).wait_recv()

    share = late_in.at[pl.ds(core * 16, 16)]
    mate_copies.append(to_mate(share, share, 1))
    mate_copies[0].wait_recv()
    near, far = factors_in[0], factors_in[1]
    near_high, near_low = halves(near)
    far_high, far_low = halves(far)
    near_product, later = [], []

    def use_near(value, part):
        put(0, value, part)
        near_product.append(value)

    times_weights(near_high, near_low, RANK, use_near)
    pl.semaphore_wait(ready_sem, SIDE - 1)
    send_over_rows(0)
    mate_copies[1].wait_recv()
    late = whole(late_in, 0)
    late_high, late_low = halves(late)
    times_weights(
        stack(late_high, far_high), stack(late_low, far_low), 2 * RANK,
        lambda value, part: later.append(value),
    )
    near_product = jnp.concatenate(near_product, axis=1)
    later = jnp.concatenate(later, axis=1)
    product_high, product_low = halves(stack(near_product, later[RANK:]))

    sized(arrived_first.at[pl.ds(0, 2 * SIDE - 1)], gram_send.at[0], gram_sem.at[0]).wait_recv()
    near_fold, far_fold = (
        (fold_got[h, 0] + fold_got[h, 1]) + (fold_got[h, 2] + fold_got[h, 3]) for h in range(2)
    )
    solved = eliminate(
        stack(
            jnp.where(narrow, near_fold, pltpu.roll(far_fold, 64, 1)),
            jnp.where(narrow, pltpu.roll(near_fold, 64, 1), far_fold),
        ),
        True,
    )
    near_inverse, far_inverse = solved[:, :32], solved[:, 64:96]
    mixing = 0.5 * stack(-solved[:, 32:64], solved[:, 96:128])
    mixing_high, mixing_low = halves(mixing)

    def mixed(high, low):
        return fast_dot(mixing_high, high, FIRST) + (
            fast_dot(mixing_high, low, FIRST) + fast_dot(mixing_low, high, FIRST)
        )

    terms = later[:RANK] + mixed(product_high, product_low)
    for part in range(4):
        put(1, terms[:, part * 256 : part * 256 + 256], part)
    send_over_rows(1)

    factor = late + mixed(stack(near_high, far_high), stack(near_low, far_low))
    factor_high, factor_low = halves(factor)
    nothing = jnp.zeros((RANK, WIDTH), jnp.bfloat16)
    block = fast_dot(
        stack(factor_high, factor_low),
        stack(
            factor_high, near_high, far_high, nothing,
            factor_low, near_low, far_low, nothing,
        ),
        LAST,
    )
    gram_start(block[:RANK, :128] + (block[:RANK, 128:] + block[RANK:, :128]))

    @pl.when(col_owner)
    def _():
        owned_over_rows(0)
        for k in range(ISLANDS):
            sums_out[k, 0] = summed[0, k] + summed[0, partner[0, k]]
        for k in range(ISLANDS):
            sums_out[k, 1] = sums_out[partner[1, k], 0]
        give_over_rows(2, sums_out, sums_in)

    left_ref[:RANK, :] = 0.5 * exact_dot(near_inverse, near, PLAIN)

    @pl.when(col_owner)
    def _():
        owned_over_rows(1)
        for k in range(ISLANDS):
            last_out[k, 0] = summed[1, k] + summed[1, partner[1, k]]
        give_over_rows(3, last_out, last_in)

    crossed = gram_finish()
    left_ref[RANK:, :] = 0.5 * exact_dot(eliminate(crossed, False)[:, :32], factor, PLAIN)
    near_change = -0.5 * exact_dot(crossed[:, 32:64], near_inverse, PLAIN)
    far_change = 0.5 * exact_dot(crossed[:, 64:96], far_inverse, PLAIN)
    sized(sums_in, back_sem.at[2], get_sem.at[2]).wait_recv()
    near_sums = whole(sums_in, 0)
    right_ref[:RANK, :] = near_sums
    change = exact_dot(
        jnp.concatenate([near_change, far_change], axis=1), stack(near_sums, whole(sums_in, 1)), PLAIN
    )
    sized(last_in, back_sem.at[3], get_sem.at[3]).wait_recv()
    right_ref[RANK:, :] = whole(last_in, 0) + change

    for copy in mate_copies:
        copy.wait_send()
    sized(arrived_first.at[pl.ds(0, 2 * SIDE - 1)], gram_send.at[0], gram_sem.at[0]).wait_send()
    sized(gram_got.at[pl.ds(0, SIDE - 1)], gram_send.at[1], gram_sem.at[1]).wait_send()
    for flow in range(2):
        sized(sent.at[flow], send_sem.at[flow + 1], own_sem.at[flow + 1]).wait_send()

    @pl.when(row_owner)
    def _():
        sized(first.at[pl.ds(0, TILES - 1)], send_sem.at[0], own_sem.at[0]).wait_send()
        sized(arrived_first.at[pl.ds(0, PEERS - 1)], back_sem.at[0], get_sem.at[0]).wait_send()

        @pl.when(late_share)
        def _():
            sized(late_in.at[pl.ds(0, 2 * ISLANDS - 1)], back_sem.at[1], get_sem.at[1]).wait_send()

        @pl.when(jnp.logical_not(late_share))
        def _():
            sized(late_in, back_sem.at[1], get_sem.at[1]).wait_send()

    @pl.when(jnp.logical_not(row_owner))
    def _():
        sized(first, send_sem.at[0], own_sem.at[0]).wait_send()

    @pl.when(col_owner)
    def _():
        for flow, count in ((2, 2), (3, 1)):
            sized(arrived.at[pl.ds(0, count)], back_sem.at[flow], get_sem.at[flow]).wait_send()


def update_kernel(weights_ref, left_ref, right_ref, out_ref, updated, sem):
    parts, rows = updated.shape[:2]
    high, low = halves(right_ref[...])
    right_stack = stack(high, low, high)
    copies = []
    for part in range(parts):
        block = pl.ds(part * rows, rows)
        high, low = halves(left_ref[:, block])
        updated[part] = weights_ref[block, :] - fast_dot(stack(high, high, low), right_stack, FIRST)
        copy = pltpu.make_async_copy(updated.at[part], out_ref.at[0, block, :], sem.at[part])
        copy.start()
        copies.append(copy)
    for copy in copies:
        copy.wait()


def shards(weights, bases, pairs):
    vmem = pl.BlockSpec(memory_space=pltpu.VMEM)
    hbm = pl.BlockSpec(memory_space=pltpu.HBM)
    factors = jax.ShapeDtypeStruct((2 * RANK, WIDTH), jnp.float32)
    tile = jax.ShapeDtypeStruct((WIDTH, WIDTH), jnp.float32)

    def tiles(*lead):
        return pltpu.VMEM((*lead, 8, 128), jnp.float32)

    dma = pltpu.SemaphoreType.DMA
    left, right, plain = pl.pallas_call(
        exchange_kernel,
        out_shape=(factors, factors, tile),
        in_specs=[hbm, hbm, pl.BlockSpec(memory_space=pltpu.SMEM)],
        out_specs=(vmem, vmem, vmem),
        scratch_shapes=[
            pltpu.VMEM((WIDTH, WIDTH), jnp.bfloat16),
            pltpu.VMEM((WIDTH, WIDTH), jnp.bfloat16),
            pltpu.VMEM((2, RANK, WIDTH), jnp.float32),
            pltpu.SMEM((2, ISLANDS), jnp.int32),
            tiles(TILES, 2), tiles(PEERS, 2),
            tiles(2, TILES), tiles(2, PEERS), tiles(2, ISLANDS),
            tiles(2, ISLANDS, 2), tiles(ISLANDS, 1), tiles(ISLANDS, 2), tiles(ISLANDS, 1),
            tiles(TILES, 2), tiles(TILES, 1), tiles(TILES, 2), tiles(TILES, 1),
            pltpu.VMEM((2, RANK, WIDTH), jnp.float32),
            pltpu.VMEM((RANK // 2, 128), jnp.float32),
            pltpu.VMEM((2, SIDE, RANK // 2, 128), jnp.float32),
            pltpu.VMEM((RANK, 128), jnp.float32),
            pltpu.VMEM((SIDE, RANK, 128), jnp.float32),
            dma((5,)), dma((3,)), dma((3,)), dma((4,)), dma((4,)), dma((2,)), dma((2,)), dma((2,)), dma((2,)),
            pltpu.SemaphoreType.REGULAR,
        ],
        compiler_params=pltpu.CompilerParams(
            collective_id=0, has_side_effects=True, vmem_limit_bytes=32 * 2**20
        ),
        name="exchange",
    )(*(pltpu.with_memory_space_constraint(x, pltpu.HBM) for x in (weights, bases, pairs.transpose(0, 2, 1))))
    parts = 8
    return pl.pallas_call(
        update_kernel,
        out_shape=jax.ShapeDtypeStruct(weights.shape, jnp.float32),
        in_specs=[vmem, vmem, vmem],
        out_specs=hbm,
        scratch_shapes=[pltpu.VMEM((parts, WIDTH // parts, WIDTH), jnp.float32), dma((parts,))],
        compiler_params=pltpu.CompilerParams(vmem_limit_bytes=20 * 2**20),
        name="update",
    )(plain, left, right)


def solution(mesh):
    in_specs = (P("island", "row", "col"), P(None, None, "col"), P())
    out_specs = P("island", "row", "col")
    return jax.shard_map(shards, mesh=mesh, in_specs=in_specs, out_specs=out_specs, check_vma=False)
```

```python
import jax
import jax.numpy as jnp
from jax import lax
from jax.experimental import pallas as pl
from jax.experimental.pallas import tpu as pltpu
from jax.sharding import PartitionSpec as P

MESH = pl.DeviceIdType.MESH
RANK = 32
WIDTH = 1024
TILES = 32
BLOCKS = WIDTH // 128
ISLANDS = 16
SIDE = 4
PEERS = ISLANDS * SIDE
BLOCK = 4
HIGHEST = lax.Precision.HIGHEST
LAST = (((1,), (1,)), ((), ()))
FIRST = (((0,), (0,)), ((), ()))
PLAIN = (((1,), (0,)), ((), ()))


def halves(array):
    high = array.astype(jnp.bfloat16)
    low = (array - high.astype(jnp.float32)).astype(jnp.bfloat16)
    return high, low


def device(island, row, col):
    return {"island": island, "row": row, "col": col}


def exact_dot(left, right, dims):
    return lax.dot_general(left, right, dims, precision=HIGHEST, preferred_element_type=jnp.float32)


def fast_dot(left, right, dims):
    return lax.dot_general(left, right, dims, preferred_element_type=jnp.float32)


def stack(*rows):
    return jnp.concatenate(rows, axis=0)


def eliminate(matrix, double):
    rows = lax.broadcasted_iota(jnp.int32, (RANK, 128), 0)
    lanes = lax.broadcasted_iota(jnp.int32, (1, 128), 1)
    position = lanes % 64 if double else lanes
    for start in range(0, RANK, BLOCK):
        pivots = range(start, start + BLOCK)
        factors = []
        for pivot in pivots:
            factor = jnp.broadcast_to(matrix[:, pivot : pivot + 1], (RANK, 128))
            if double:
                second = jnp.broadcast_to(matrix[:, 64 + pivot : 65 + pivot], (RANK, 128))
                factor = jnp.where(lanes < 64, factor, second)
            factors.append(factor)
        here = (position >= start) & (position < start + BLOCK)
        solved = [
            jnp.where(here, jnp.where(position == pivot, 1.0, 0.0), matrix[pivot : pivot + 1])
            for pivot in pivots
        ]
        corner = [[factor[pivot : pivot + 1] for factor in factors] for pivot in pivots]
        for j in range(BLOCK):
            scale = 1.0 / corner[j][j]
            solved[j] = solved[j] * scale
            corner[j] = [entry * scale if m > j else entry for m, entry in enumerate(corner[j])]
            for i in range(j + 1, BLOCK):
                solved[i] = solved[i] - corner[i][j] * solved[j]
                corner[i] = [
                    entry - corner[i][j] * corner[j][m] if m > j else entry
                    for m, entry in enumerate(corner[i])
                ]
        for j in reversed(range(BLOCK)):
            for i in range(j):
                solved[i] = solved[i] - corner[i][j] * solved[j]
        rest = jnp.where(here, 0.0, matrix)
        for factor, row in zip(factors, solved):
            rest = rest - factor * row
        for pivot, row in zip(pivots, solved):
            rest = jnp.where(rows == pivot, row, rest)
        matrix = rest
    return matrix


def exchange_kernel(
    weights_ref, bases_ref, pairs_ref, left_ref, right_ref, plain,
    high_ref, low_ref, bases_in, partner, first, arrived_first, sent, arrived, summed,
    pair_out, late_out, sums_out, last_out, pair_in, late_in, sums_in, last_in,
    factors_in, fold_sent, fold_got, gram_sent, gram_got,
    load_sem, send_sem, own_sem, back_sem, get_sem, mate_send, mate_sem, pass_send, pass_sem, gram_send, gram_sem, ready_sem,
):
    island, row, col = (lax.axis_index(name) for name in ("island", "row", "col"))
    side, core = col // 2, col % 2
    other = (1 - side) * 2 + core
    mate = side * 2 + 1 - core

    base_load = pltpu.make_async_copy(bases_ref, bases_in, load_sem.at[4])
    base_load.start()
    loads = []
    for part in range(4):
        rows = pl.ds(part * 256, 256)
        load = pltpu.make_async_copy(
            weights_ref.at[0, rows, :], plain.at[rows, :], load_sem.at[part]
        )
        load.start()
        loads.append(load)

    barrier = pltpu.get_barrier_semaphore()
    across, along = island // SIDE, island % SIDE

    def far_first(index):
        return (2 + 3 * index + 3 * (index * (index - 1) // 2)) % SIDE

    def far_island(index):
        return (across + far_first(index // SIDE)) % SIDE * SIDE + (along + far_first(index % SIDE)) % SIDE

    def greet(index, carry):
        k = far_island(index)
        for m in range(SIDE):

            @pl.when((k != island) | (m != col))
            def _():
                pl.semaphore_signal(barrier, inc=1, device_id=device(k, row, m), device_id_type=MESH)

        return carry

    lax.fori_loop(0, ISLANDS, greet, 0, unroll=True)
    for step in range(1, SIDE):
        pl.semaphore_signal(
            barrier, inc=1, device_id=device(island, (row + step) % SIDE, col), device_id_type=MESH
        )

    base_load.wait()
    base_high, base_low = halves(bases_in[...].reshape(2 * RANK, WIDTH))
    base_stack = stack(base_high, base_low)

    def put_first(value, part):
        for basis in range(2):
            for a in range(4):
                for b in range(2):
                    first[a * BLOCKS + part * 2 + b, basis] = value[
                        basis * RANK + a * 8 : basis * RANK + a * 8 + 8, b * 128 : b * 128 + 128
                    ]

    def put(flow, value, part):
        for a in range(4):
            for b in range(2):
                sent[flow, a * BLOCKS + part * 2 + b] = value[a * 8 : a * 8 + 8, b * 128 : b * 128 + 128]

    for part in range(4):
        loads[part].wait()
        rows = pl.ds(part * 256, 256)
        high, low = halves(plain[rows, :])
        high_ref[rows, :] = high
        low_ref[rows, :] = low
        wide = fast_dot(base_stack, high, LAST)
        fine = fast_dot(base_high, low, LAST)
        terms = wide[: 2 * RANK] + (wide[2 * RANK :] + fine)
        put_first(terms, part)

    pl.semaphore_wait(barrier, PEERS - 1 + SIDE - 1)
    for step in range(1, SIDE):
        pl.semaphore_signal(
            ready_sem, inc=1, device_id=device(island, (row + step) % SIDE, col), device_id_type=MESH
        )

    row_owner = core == island % 2
    row_tile = island * 2 + side
    col_owner = row % 2 == (island + core) % 2
    col_tile = island * 2 + row // 2

    def sized(ref, send, recv):
        return pltpu.make_async_remote_copy(
            ref, ref, send, recv, device_id=device(island, row, other), device_id_type=MESH
        )

    def add_up(flow):
        for k in range(ISLANDS):
            summed[flow, k] = (arrived[flow, k * 4] + arrived[flow, k * 4 + 1]) + (
                arrived[flow, k * 4 + 2] + arrived[flow, k * 4 + 3]
            )

    def send_over_columns():
        def send(index, carry):
            k = far_island(index)
            for which in range(2):
                m = which * 2 + k % 2

                @pl.when((k != island) | (m != col))
                def _():
                    pltpu.make_async_remote_copy(
                        first.at[2 * k + which], arrived_first.at[island * 4 + col],
                        send_sem.at[0], own_sem.at[0],
                        device_id=device(k, row, m), device_id_type=MESH,
                    ).start()

            return carry

        lax.fori_loop(0, ISLANDS, send, 0, unroll=True)

    def give_pairs():
        def give(index, carry):
            k = far_island(index)
            for m in range(SIDE):

                @pl.when((k != island) | (m != col))
                def _():
                    pltpu.make_async_remote_copy(
                        pair_out.at[m % 2, k], pair_in.at[row_tile], back_sem.at[0], get_sem.at[0],
                        device_id=device(k, row, m), device_id_type=MESH,
                    ).start()

            return carry

        lax.fori_loop(0, ISLANDS, give, 0, unroll=True)
        pair_in[row_tile] = pair_out[core, island]

    def give_late():
        def give(index, carry):
            k = far_island(index)
            for half in range(2):
                m = half * 2 + row_tile // 16

                @pl.when((k != island) | (m != col))
                def _():
                    pltpu.make_async_remote_copy(
                        late_out.at[k], late_in.at[row_tile], back_sem.at[1], get_sem.at[1],
                        device_id=device(k, row, m), device_id_type=MESH,
                    ).start()

            return carry

        lax.fori_loop(0, ISLANDS, give, 0, unroll=True)

        @pl.when(row_tile // 16 == core)
        def _():
            late_in[row_tile] = late_out[island]

    def send_over_rows(flow):
        def send(index, carry):
            k = far_island(index)
            for which in range(2):
                pltpu.make_async_remote_copy(
                    sent.at[flow, 2 * k + which], arrived.at[flow, island * 4 + row],
                    send_sem.at[flow + 1], own_sem.at[flow + 1],
                    device_id=device(k, which * 2 + (k + core) % 2, other), device_id_type=MESH,
                ).start()
            return carry

        lax.fori_loop(0, ISLANDS, send, 0, unroll=True)

    def owned_over_rows(flow):
        sized(arrived.at[flow], send_sem.at[flow + 1], own_sem.at[flow + 1]).wait_recv()
        add_up(flow)

    def give_over_rows(flow, out, into):
        def give(index, carry):
            k = far_island(index % ISLANDS)
            for near in range(2):
                m = (row + 1 + side + near + 2 * (index // ISLANDS)) % SIDE
                pltpu.make_async_remote_copy(
                    out.at[k], into.at[col_tile], back_sem.at[flow], get_sem.at[flow],
                    device_id=device(k, m, other), device_id_type=MESH,
                ).start()
            return carry

        lax.fori_loop(0, 2 * ISLANDS, give, 0, unroll=True)

    def whole(ref, which):
        return stack(
            *(
                jnp.concatenate([ref[a * BLOCKS + b, which] for b in range(BLOCKS)], axis=1)
                for a in range(4)
            )
        )

    def to_mate(source, target, index):
        copy = pltpu.make_async_remote_copy(
            source, target, mate_send.at[index], mate_sem.at[index],
            device_id=device(island, row, mate), device_id_type=MESH,
        )
        copy.start()
        return copy

    def gram_start(gram):
        gram_sent[...] = gram
        gram_got[row] = gram
        for step in range(1, SIDE):
            pltpu.make_async_remote_copy(
                gram_sent, gram_got.at[row], gram_send.at[1], gram_sem.at[1],
                device_id=device(island, (row + step) % SIDE, col), device_id_type=MESH,
            ).start()

    def gram_finish():
        sized(gram_got.at[pl.ds(0, SIDE - 1)], gram_send.at[1], gram_sem.at[1]).wait_recv()
        return (gram_got[0] + gram_got[1]) + (gram_got[2] + gram_got[3])

    def times_weights(high, low, count, use):
        both = stack(high, low)
        for part in range(4):
            cols = pl.ds(part * 256, 256)
            wide = fast_dot(both, high_ref[:, cols], PLAIN)
            fine = fast_dot(high, low_ref[:, cols], PLAIN)
            use(wide[:count] + (wide[count:] + fine), part)

    send_over_columns()

    def find(index, carry):
        for matching in range(2):
            found = jnp.int32(0)
            for pair in range(ISLANDS // 2):
                first, second = pairs_ref[matching, 0, pair], pairs_ref[matching, 1, pair]
                found += jnp.where(first == index, second, 0) + jnp.where(second == index, first, 0)
            partner[matching, index] = found
        return carry

    lax.fori_loop(0, ISLANDS, find, 0)

    @pl.when(row_owner)
    def _():
        arrived_first[island * 4 + col] = first[row_tile]
        sized(arrived_first.at[pl.ds(0, PEERS - 1)], send_sem.at[0], own_sem.at[0]).wait_recv()
        for k in range(ISLANDS):
            for basis in range(2):
                summed[basis, k] = (
                    arrived_first[k * 4, basis] + arrived_first[k * 4 + 1, basis]
                ) + (arrived_first[k * 4 + 2, basis] + arrived_first[k * 4 + 3, basis])
        for k in range(ISLANDS):
            for basis in range(2):
                pair_out[0, k, basis] = summed[basis, k] - summed[basis, partner[0, k]]
        for k in range(ISLANDS):
            pair_out[1, k] = pair_out[0, partner[1, k]]
        give_pairs()
        for k in range(ISLANDS):
            late_out[k, 0] = summed[1, k] - summed[1, partner[1, k]]
        give_late()
        sized(pair_in.at[pl.ds(0, TILES - 1)], back_sem.at[0], get_sem.at[0]).wait_recv()

    @pl.when(jnp.logical_not(row_owner))
    def _():
        sized(pair_in, back_sem.at[0], get_sem.at[0]).wait_recv()

    mine = whole(pair_in, 0)
    factors_in[core] = mine
    mate_copies = [to_mate(factors_in.at[core], factors_in.at[core], 0)]
    mine_high, mine_low = halves(mine)
    cross_high, cross_low = halves(whole(pair_in, 1))
    block = fast_dot(
        stack(mine_high, mine_low),
        stack(mine_high, cross_high, mine_high, cross_high, mine_low, cross_low, mine_low, cross_low),
        LAST,
    )
    block = block[:RANK, :128] + (block[:RANK, 128:] + block[RANK:, :128])
    narrow = lax.broadcasted_iota(jnp.int32, (RANK // 2, 128), 1) < 64
    fold_sent[...] = jnp.where(narrow, block[: RANK // 2], block[RANK // 2 :])
    fold_got[core, row] = fold_sent[...]

    def fold(index, carry):
        m, h = (row + 1 + index // 2) % SIDE, index % 2

        @pl.when((m != row) | (h != core))
        def _():
            pltpu.make_async_remote_copy(
                fold_sent, fold_got.at[core, row], gram_send.at[0], gram_sem.at[0],
                device_id=device(island, m, side * 2 + h), device_id_type=MESH,
            ).start()

        return carry

    lax.fori_loop(0, 2 * SIDE, fold, 0)

    late_share = row_owner & (row_tile // 16 == core)

    @pl.when(late_share)
    def _():
        sized(late_in.at[pl.ds(0, TILES // 2 - 1)], back_sem.at[1], get_sem.at[1]).wait_recv()

    @pl.when(jnp.logical_not(late_share))
    def _():
        sized(late_in.at[pl.ds(0, TILES // 2)], back_sem.at[1], get_sem.at[1]).wait_recv()

    share = late_in.at[pl.ds(core * 16, 16)]
    mate_copies.append(to_mate(share, share, 1))
    mate_copies[0].wait_recv()
    near, far = factors_in[0], factors_in[1]
    near_high, near_low = halves(near)
    far_high, far_low = halves(far)
    near_product, later = [], []

    def use_near(value, part):
        put(0, value, part)
        near_product.append(value)

    times_weights(near_high, near_low, RANK, use_near)
    pl.semaphore_wait(ready_sem, SIDE - 1)
    send_over_rows(0)
    mate_copies[1].wait_recv()
    late = whole(late_in, 0)
    late_high, late_low = halves(late)
    times_weights(
        stack(late_high, far_high), stack(late_low, far_low), 2 * RANK,
        lambda value, part: later.append(value),
    )
    near_product = jnp.concatenate(near_product, axis=1)
    later = jnp.concatenate(later, axis=1)
    product_high, product_low = halves(stack(near_product, later[RANK:]))

    sized(arrived_first.at[pl.ds(0, 2 * SIDE - 1)], gram_send.at[0], gram_sem.at[0]).wait_recv()
    near_fold, far_fold = (
        (fold_got[h, 0] + fold_got[h, 1]) + (fold_got[h, 2] + fold_got[h, 3]) for h in range(2)
    )
    solved = eliminate(
        stack(
            jnp.where(narrow, near_fold, pltpu.roll(far_fold, 64, 1)),
            jnp.where(narrow, pltpu.roll(near_fold, 64, 1), far_fold),
        ),
        True,
    )
    near_inverse, far_inverse = solved[:, :32], solved[:, 64:96]
    mixing = 0.5 * stack(-solved[:, 32:64], solved[:, 96:128])
    mixing_high, mixing_low = halves(mixing)

    def mixed(high, low):
        return fast_dot(mixing_high, high, FIRST) + (
            fast_dot(mixing_high, low, FIRST) + fast_dot(mixing_low, high, FIRST)
        )

    terms = later[:RANK] + mixed(product_high, product_low)
    for part in range(4):
        put(1, terms[:, part * 256 : part * 256 + 256], part)
    send_over_rows(1)

    factor = late + mixed(stack(near_high, far_high), stack(near_low, far_low))
    factor_high, factor_low = halves(factor)
    nothing = jnp.zeros((RANK, WIDTH), jnp.bfloat16)
    block = fast_dot(
        stack(factor_high, factor_low),
        stack(
            factor_high, near_high, far_high, nothing,
            factor_low, near_low, far_low, nothing,
        ),
        LAST,
    )
    gram_start(block[:RANK, :128] + (block[:RANK, 128:] + block[RANK:, :128]))

    @pl.when(col_owner)
    def _():
        owned_over_rows(0)
        for k in range(ISLANDS):
            sums_out[k, 0] = summed[0, k] + summed[0, partner[0, k]]
        for k in range(ISLANDS):
            sums_out[k, 1] = sums_out[partner[1, k], 0]

        def give(index, carry):
            k = far_island(index)
            for near in range(2):
                m = (row + 3 + side + near) % SIDE
                pltpu.make_async_remote_copy(
                    sums_out.at[k], sums_in.at[row, island // 2], back_sem.at[2], get_sem.at[2],
                    device_id=device(k, m, other), device_id_type=MESH,
                ).start()
            return carry

        lax.fori_loop(0, ISLANDS, give, 0, unroll=True)


    left_ref[:RANK, :] = 0.5 * exact_dot(near_inverse, near, PLAIN)

    @pl.when(col_owner)
    def _():
        owned_over_rows(1)
        for k in range(ISLANDS):
            last_out[k, 0] = summed[1, k] + summed[1, partner[1, k]]
        give_over_rows(3, last_out, last_in)

    sized(arrived.at[0, pl.ds(0, TILES)], back_sem.at[2], get_sem.at[2]).wait_recv()
    passed = []
    for index, (source, target) in enumerate(
        (((row + side) % SIDE, (row + 3) % SIDE), ((row + side + 3) % SIDE, (row + 1) % SIDE))
    ):
        copy = pltpu.make_async_remote_copy(
            sums_in.at[source], sums_in.at[source], pass_send.at[index], pass_sem.at[index],
            device_id=device(island, target, col), device_id_type=MESH,
        )
        copy.start()
        passed.append(copy)

    def whole_sums(which):
        def tile(index):
            k = index // 2
            return sums_in[index % 2 * 2 + (k + core) % 2, k // 2, which]

        return stack(
            *(
                jnp.concatenate([tile(a * BLOCKS + b) for b in range(BLOCKS)], axis=1)
                for a in range(4)
            )
        )

    crossed = gram_finish()
    left_ref[RANK:, :] = 0.5 * exact_dot(eliminate(crossed, False)[:, :32], factor, PLAIN)
    near_change = -0.5 * exact_dot(crossed[:, 32:64], near_inverse, PLAIN)
    far_change = 0.5 * exact_dot(crossed[:, 64:96], far_inverse, PLAIN)
    for copy in passed:
        copy.wait_recv()
    near_sums = whole_sums(0)
    right_ref[:RANK, :] = near_sums
    change_high, change_low = halves(jnp.concatenate([near_change, far_change], axis=1))
    sums_high, sums_low = halves(stack(near_sums, whole_sums(1)))
    change = fast_dot(change_high, sums_high, PLAIN) + (
        fast_dot(change_high, sums_low, PLAIN) + fast_dot(change_low, sums_high, PLAIN)
    )
    sized(last_in, back_sem.at[3], get_sem.at[3]).wait_recv()
    right_ref[RANK:, :] = whole(last_in, 0) + change

    for copy in mate_copies + passed:
        copy.wait_send()
    sized(arrived_first.at[pl.ds(0, 2 * SIDE - 1)], gram_send.at[0], gram_sem.at[0]).wait_send()
    sized(gram_got.at[pl.ds(0, SIDE - 1)], gram_send.at[1], gram_sem.at[1]).wait_send()
    for flow in range(2):
        sized(sent.at[flow], send_sem.at[flow + 1], own_sem.at[flow + 1]).wait_send()

    @pl.when(row_owner)
    def _():
        sized(first.at[pl.ds(0, TILES - 1)], send_sem.at[0], own_sem.at[0]).wait_send()
        sized(arrived_first.at[pl.ds(0, PEERS - 1)], back_sem.at[0], get_sem.at[0]).wait_send()

        @pl.when(late_share)
        def _():
            sized(late_in.at[pl.ds(0, 2 * ISLANDS - 1)], back_sem.at[1], get_sem.at[1]).wait_send()

        @pl.when(jnp.logical_not(late_share))
        def _():
            sized(late_in, back_sem.at[1], get_sem.at[1]).wait_send()

    @pl.when(jnp.logical_not(row_owner))
    def _():
        sized(first, send_sem.at[0], own_sem.at[0]).wait_send()

    @pl.when(col_owner)
    def _():
        for flow in (2, 3):
            sized(arrived.at[0], back_sem.at[flow], get_sem.at[flow]).wait_send()


def update_kernel(weights_ref, left_ref, right_ref, out_ref, updated, sem):
    parts, rows = updated.shape[:2]
    high, low = halves(right_ref[...])
    right_stack = stack(high, low, high)
    copies = []
    for part in range(parts):
        block = pl.ds(part * rows, rows)
        high, low = halves(left_ref[:, block])
        updated[part] = weights_ref[block, :] - fast_dot(stack(high, high, low), right_stack, FIRST)
        copy = pltpu.make_async_copy(updated.at[part], out_ref.at[0, block, :], sem.at[part])
        copy.start()
        copies.append(copy)
    for copy in copies:
        copy.wait()


def shards(weights, bases, pairs):
    vmem = pl.BlockSpec(memory_space=pltpu.VMEM)
    hbm = pl.BlockSpec(memory_space=pltpu.HBM)
    factors = jax.ShapeDtypeStruct((2 * RANK, WIDTH), jnp.float32)
    tile = jax.ShapeDtypeStruct((WIDTH, WIDTH), jnp.float32)

    def tiles(*lead):
        return pltpu.VMEM((*lead, 8, 128), jnp.float32)

    dma = pltpu.SemaphoreType.DMA
    left, right, plain = pl.pallas_call(
        exchange_kernel,
        out_shape=(factors, factors, tile),
        in_specs=[hbm, hbm, pl.BlockSpec(memory_space=pltpu.SMEM)],
        out_specs=(vmem, vmem, vmem),
        scratch_shapes=[
            pltpu.VMEM((WIDTH, WIDTH), jnp.bfloat16),
            pltpu.VMEM((WIDTH, WIDTH), jnp.bfloat16),
            pltpu.VMEM((2, RANK, WIDTH), jnp.float32),
            pltpu.SMEM((2, ISLANDS), jnp.int32),
            tiles(TILES, 2), tiles(PEERS, 2),
            tiles(2, TILES), tiles(2, PEERS), tiles(2, ISLANDS),
            tiles(2, ISLANDS, 2), tiles(ISLANDS, 1), tiles(ISLANDS, 2), tiles(ISLANDS, 1),
            tiles(TILES, 2), tiles(TILES, 1), tiles(SIDE, TILES // SIDE, 2), tiles(TILES, 1),
            pltpu.VMEM((2, RANK, WIDTH), jnp.float32),
            pltpu.VMEM((RANK // 2, 128), jnp.float32),
            pltpu.VMEM((2, SIDE, RANK // 2, 128), jnp.float32),
            pltpu.VMEM((RANK, 128), jnp.float32),
            pltpu.VMEM((SIDE, RANK, 128), jnp.float32),
            dma((5,)), dma((3,)), dma((3,)), dma((4,)), dma((4,)), dma((2,)), dma((2,)), dma((2,)), dma((2,)), dma((2,)), dma((2,)),
            pltpu.SemaphoreType.REGULAR,
        ],
        compiler_params=pltpu.CompilerParams(
            collective_id=0, has_side_effects=True, vmem_limit_bytes=32 * 2**20
        ),
        name="exchange",
    )(*(pltpu.with_memory_space_constraint(x, pltpu.HBM) for x in (weights, bases, pairs.transpose(0, 2, 1))))
    parts = 8
    return pl.pallas_call(
        update_kernel,
        out_shape=jax.ShapeDtypeStruct(weights.shape, jnp.float32),
        in_specs=[vmem, vmem, vmem],
        out_specs=hbm,
        scratch_shapes=[pltpu.VMEM((parts, WIDTH // parts, WIDTH), jnp.float32), dma((parts,))],
        compiler_params=pltpu.CompilerParams(vmem_limit_bytes=20 * 2**20),
        name="update",
    )(plain, left, right)


def solution(mesh):
    in_specs = (P("island", "row", "col"), P(None, None, "col"), P())
    out_specs = P("island", "row", "col")
    return jax.shard_map(shards, mesh=mesh, in_specs=in_specs, out_specs=out_specs, check_vma=False)
```

```python
import jax
import jax.numpy as jnp
from jax import lax
from jax.experimental import pallas as pl
from jax.experimental.pallas import tpu as pltpu
from jax.sharding import PartitionSpec as P

MESH = pl.DeviceIdType.MESH
RANK = 32
WIDTH = 1024
TILES = 32
BLOCKS = WIDTH // 128
ISLANDS = 16
SIDE = 4
PEERS = ISLANDS * SIDE
BLOCK = 8
HIGHEST = lax.Precision.HIGHEST
LAST = (((1,), (1,)), ((), ()))
FIRST = (((0,), (0,)), ((), ()))
PLAIN = (((1,), (0,)), ((), ()))


def halves(array):
    high = array.astype(jnp.bfloat16)
    low = (array - high.astype(jnp.float32)).astype(jnp.bfloat16)
    return high, low


def device(island, row, col):
    return {"island": island, "row": row, "col": col}


def exact_dot(left, right, dims):
    return lax.dot_general(left, right, dims, precision=HIGHEST, preferred_element_type=jnp.float32)


def fast_dot(left, right, dims):
    return lax.dot_general(left, right, dims, preferred_element_type=jnp.float32)


def stack(*rows):
    return jnp.concatenate(rows, axis=0)


def eliminate(matrix, double):
    rows = lax.broadcasted_iota(jnp.int32, (RANK, 128), 0)
    lanes = lax.broadcasted_iota(jnp.int32, (1, 128), 1)
    position = lanes % 64 if double else lanes
    for start in range(0, RANK, BLOCK):
        pivots = range(start, start + BLOCK)
        factors = []
        for pivot in pivots:
            factor = jnp.broadcast_to(matrix[:, pivot : pivot + 1], (RANK, 128))
            if double:
                second = jnp.broadcast_to(matrix[:, 64 + pivot : 65 + pivot], (RANK, 128))
                factor = jnp.where(lanes < 64, factor, second)
            factors.append(factor)
        here = (position >= start) & (position < start + BLOCK)
        solved = [
            jnp.where(here, jnp.where(position == pivot, 1.0, 0.0), matrix[pivot : pivot + 1])
            for pivot in pivots
        ]
        corner = [[factor[pivot : pivot + 1] for factor in factors] for pivot in pivots]
        for j in range(BLOCK):
            scale = 1.0 / corner[j][j]
            solved[j] = solved[j] * scale
            corner[j] = [entry * scale if m > j else entry for m, entry in enumerate(corner[j])]
            for i in range(j + 1, BLOCK):
                solved[i] = solved[i] - corner[i][j] * solved[j]
                corner[i] = [
                    entry - corner[i][j] * corner[j][m] if m > j else entry
                    for m, entry in enumerate(corner[i])
                ]
        for j in reversed(range(BLOCK)):
            for i in range(j):
                solved[i] = solved[i] - corner[i][j] * solved[j]
        rest = jnp.where(here, 0.0, matrix)
        for factor, row in zip(factors, solved):
            rest = rest - factor * row
        for pivot, row in zip(pivots, solved):
            rest = jnp.where(rows == pivot, row, rest)
        matrix = rest
    return matrix


def exchange_kernel(
    weights_ref, bases_ref, pairs_ref, left_ref, right_ref, plain,
    high_ref, low_ref, bases_in, partner, first, arrived_first, sent, arrived, summed,
    pair_out, late_out, sums_out, last_out, pair_in, late_in, sums_in, last_in,
    factors_in, fold_sent, fold_got, gram_sent, gram_got,
    load_sem, send_sem, own_sem, back_sem, get_sem, mate_send, mate_sem, pass_send, pass_sem, gram_send, gram_sem,
):
    island, row, col = (lax.axis_index(name) for name in ("island", "row", "col"))
    side, core = col // 2, col % 2
    other = (1 - side) * 2 + core
    mate = side * 2 + 1 - core

    base_load = pltpu.make_async_copy(bases_ref, bases_in, load_sem.at[4])
    base_load.start()
    loads = []
    for part in range(4):
        rows = pl.ds(part * 256, 256)
        load = pltpu.make_async_copy(
            weights_ref.at[0, rows, :], plain.at[rows, :], load_sem.at[part]
        )
        load.start()
        loads.append(load)

    barrier = pltpu.get_barrier_semaphore()
    across, along = island // SIDE, island % SIDE

    def far_first(index):
        return (2 + 3 * index + 3 * (index * (index - 1) // 2)) % SIDE

    def far_island(index):
        return (across + far_first(index // SIDE)) % SIDE * SIDE + (along + far_first(index % SIDE)) % SIDE

    row_owner = core == island % 2

    @pl.when(row_owner)
    def _():
        def greet(index, carry):
            k = far_island(index)
            for m in range(SIDE):

                @pl.when((k != island) | (m != col))
                def _():
                    pl.semaphore_signal(barrier, inc=1, device_id=device(k, row, m), device_id_type=MESH)

            return carry

        lax.fori_loop(0, ISLANDS, greet, 0, unroll=True)

    for step in range(1, SIDE):
        pl.semaphore_signal(
            barrier, inc=1, device_id=device(island, (row + step) % SIDE, col), device_id_type=MESH
        )

    base_load.wait()
    base_high, base_low = halves(bases_in[...].reshape(2 * RANK, WIDTH))
    base_stack = stack(base_high, base_low)

    def put_first(value, part):
        for basis in range(2):
            for a in range(4):
                for b in range(2):
                    first[a * BLOCKS + part * 2 + b, basis] = value[
                        basis * RANK + a * 8 : basis * RANK + a * 8 + 8, b * 128 : b * 128 + 128
                    ]

    def put(flow, value, part):
        for a in range(4):
            for b in range(2):
                sent[flow, a * BLOCKS + part * 2 + b] = value[a * 8 : a * 8 + 8, b * 128 : b * 128 + 128]

    for part in range(4):
        loads[part].wait()
        rows = pl.ds(part * 256, 256)
        high, low = halves(plain[rows, :])
        high_ref[rows, :] = high
        low_ref[rows, :] = low
        wide = fast_dot(base_stack, high, LAST)
        fine = fast_dot(base_high, low, LAST)
        terms = wide[: 2 * RANK] + (wide[2 * RANK :] + fine)
        put_first(terms, part)

    pl.semaphore_wait(barrier, TILES - row_owner.astype(jnp.int32) + SIDE - 1)

    row_tile = island * 2 + side
    col_owner = row % 2 == (island + core) % 2
    col_tile = island * 2 + row // 2

    def sized(ref, send, recv):
        return pltpu.make_async_remote_copy(
            ref, ref, send, recv, device_id=device(island, row, other), device_id_type=MESH
        )

    def add_up(flow):
        for k in range(ISLANDS):
            summed[flow, k] = (arrived[flow, k * 4] + arrived[flow, k * 4 + 1]) + (
                arrived[flow, k * 4 + 2] + arrived[flow, k * 4 + 3]
            )

    def send_over_columns():
        def send(index, carry):
            k = far_island(index)
            for which in range(2):
                m = which * 2 + k % 2

                @pl.when((k != island) | (m != col))
                def _():
                    pltpu.make_async_remote_copy(
                        first.at[2 * k + which], arrived_first.at[island * 4 + col],
                        send_sem.at[0], own_sem.at[0],
                        device_id=device(k, row, m), device_id_type=MESH,
                    ).start()

            return carry

        lax.fori_loop(0, ISLANDS, send, 0, unroll=True)

    def give_pairs():
        def give(index, carry):
            k = far_island(index)
            for m in range(SIDE):

                @pl.when((k != island) | (m != col))
                def _():
                    pltpu.make_async_remote_copy(
                        pair_out.at[m % 2, k], pair_in.at[row_tile], back_sem.at[0], get_sem.at[0],
                        device_id=device(k, row, m), device_id_type=MESH,
                    ).start()

            return carry

        lax.fori_loop(0, ISLANDS, give, 0, unroll=True)
        pair_in[row_tile] = pair_out[core, island]

    def give_late():
        def give(index, carry):
            k = far_island(index)
            for half in range(2):
                m = half * 2 + row_tile // 16

                @pl.when((k != island) | (m != col))
                def _():
                    pltpu.make_async_remote_copy(
                        late_out.at[k], late_in.at[row_tile], back_sem.at[1], get_sem.at[1],
                        device_id=device(k, row, m), device_id_type=MESH,
                    ).start()

            return carry

        lax.fori_loop(0, ISLANDS, give, 0, unroll=True)

        @pl.when(row_tile // 16 == core)
        def _():
            late_in[row_tile] = late_out[island]

    def send_over_rows(flow):
        def send(index, carry):
            k = far_island(index)
            for which in range(2):
                pltpu.make_async_remote_copy(
                    sent.at[flow, 2 * k + which], arrived.at[flow, island * 4 + row],
                    send_sem.at[flow + 1], own_sem.at[flow + 1],
                    device_id=device(k, which * 2 + (k + core) % 2, other), device_id_type=MESH,
                ).start()
            return carry

        lax.fori_loop(0, ISLANDS, send, 0, unroll=True)

    def owned_over_rows(flow):
        sized(arrived.at[flow], send_sem.at[flow + 1], own_sem.at[flow + 1]).wait_recv()
        add_up(flow)

    def give_over_rows(flow, out, into):
        def give(index, carry):
            k = far_island(index % ISLANDS)
            for near in range(2):
                m = (row + 1 + side + near + 2 * (index // ISLANDS)) % SIDE
                pltpu.make_async_remote_copy(
                    out.at[k], into.at[col_tile], back_sem.at[flow], get_sem.at[flow],
                    device_id=device(k, m, other), device_id_type=MESH,
                ).start()
            return carry

        lax.fori_loop(0, 2 * ISLANDS, give, 0, unroll=True)

    def whole(ref, which):
        return stack(
            *(
                jnp.concatenate([ref[a * BLOCKS + b, which] for b in range(BLOCKS)], axis=1)
                for a in range(4)
            )
        )

    def to_mate(source, target, index):
        copy = pltpu.make_async_remote_copy(
            source, target, mate_send.at[index], mate_sem.at[index],
            device_id=device(island, row, mate), device_id_type=MESH,
        )
        copy.start()
        return copy

    def gram_start(gram):
        gram_sent[...] = gram
        gram_got[row] = gram
        for step in range(1, SIDE):
            pltpu.make_async_remote_copy(
                gram_sent, gram_got.at[row], gram_send.at[1], gram_sem.at[1],
                device_id=device(island, (row + step) % SIDE, col), device_id_type=MESH,
            ).start()

    def gram_finish():
        sized(gram_got.at[pl.ds(0, SIDE - 1)], gram_send.at[1], gram_sem.at[1]).wait_recv()
        return (gram_got[0] + gram_got[1]) + (gram_got[2] + gram_got[3])

    def times_weights(high, low, count, use):
        both = stack(high, low)
        for part in range(4):
            cols = pl.ds(part * 256, 256)
            wide = fast_dot(both, high_ref[:, cols], PLAIN)
            fine = fast_dot(high, low_ref[:, cols], PLAIN)
            use(wide[:count] + (wide[count:] + fine), part)

    send_over_columns()

    def find(index, carry):
        for matching in range(2):
            found = jnp.int32(0)
            for pair in range(ISLANDS // 2):
                first, second = pairs_ref[matching, 0, pair], pairs_ref[matching, 1, pair]
                found += jnp.where(first == index, second, 0) + jnp.where(second == index, first, 0)
            partner[matching, index] = found
        return carry

    lax.fori_loop(0, ISLANDS, find, 0)

    @pl.when(row_owner)
    def _():
        arrived_first[island * 4 + col] = first[row_tile]
        sized(arrived_first.at[pl.ds(0, PEERS - 1)], send_sem.at[0], own_sem.at[0]).wait_recv()
        for k in range(ISLANDS):
            for basis in range(2):
                summed[basis, k] = (
                    arrived_first[k * 4, basis] + arrived_first[k * 4 + 1, basis]
                ) + (arrived_first[k * 4 + 2, basis] + arrived_first[k * 4 + 3, basis])
        for k in range(ISLANDS):
            for basis in range(2):
                pair_out[0, k, basis] = summed[basis, k] - summed[basis, partner[0, k]]
        for k in range(ISLANDS):
            pair_out[1, k] = pair_out[0, partner[1, k]]
        give_pairs()
        for k in range(ISLANDS):
            late_out[k, 0] = summed[1, k] - summed[1, partner[1, k]]
        give_late()
        sized(pair_in.at[pl.ds(0, TILES - 1)], back_sem.at[0], get_sem.at[0]).wait_recv()

    @pl.when(jnp.logical_not(row_owner))
    def _():
        sized(pair_in, back_sem.at[0], get_sem.at[0]).wait_recv()

    mine = whole(pair_in, 0)
    factors_in[core] = mine
    mate_copies = [to_mate(factors_in.at[core], factors_in.at[core], 0)]
    mine_high, mine_low = halves(mine)
    cross_high, cross_low = halves(whole(pair_in, 1))
    block = fast_dot(
        stack(mine_high, mine_low),
        stack(mine_high, cross_high, mine_high, cross_high, mine_low, cross_low, mine_low, cross_low),
        LAST,
    )
    block = block[:RANK, :128] + (block[:RANK, 128:] + block[RANK:, :128])
    narrow = lax.broadcasted_iota(jnp.int32, (RANK // 2, 128), 1) < 64
    fold_sent[...] = jnp.where(narrow, block[: RANK // 2], block[RANK // 2 :])
    fold_got[core, row] = fold_sent[...]

    def fold(index, carry):
        m, h = (row + 1 + index // 2) % SIDE, index % 2

        @pl.when((m != row) | (h != core))
        def _():
            pltpu.make_async_remote_copy(
                fold_sent, fold_got.at[core, row], gram_send.at[0], gram_sem.at[0],
                device_id=device(island, m, side * 2 + h), device_id_type=MESH,
            ).start()

        return carry

    lax.fori_loop(0, 2 * SIDE, fold, 0)

    late_share = row_owner & (row_tile // 16 == core)

    @pl.when(late_share)
    def _():
        sized(late_in.at[pl.ds(0, TILES // 2 - 1)], back_sem.at[1], get_sem.at[1]).wait_recv()

    @pl.when(jnp.logical_not(late_share))
    def _():
        sized(late_in.at[pl.ds(0, TILES // 2)], back_sem.at[1], get_sem.at[1]).wait_recv()

    share = late_in.at[pl.ds(core * 16, 16)]
    mate_copies.append(to_mate(share, share, 1))
    mate_copies[0].wait_recv()
    near, far = factors_in[0], factors_in[1]
    near_high, near_low = halves(near)
    far_high, far_low = halves(far)
    near_product, later = [], []

    def use_near(value, part):
        put(0, value, part)
        near_product.append(value)

    times_weights(near_high, near_low, RANK, use_near)
    send_over_rows(0)
    mate_copies[1].wait_recv()
    late = whole(late_in, 0)
    late_high, late_low = halves(late)
    times_weights(
        stack(late_high, far_high), stack(late_low, far_low), 2 * RANK,
        lambda value, part: later.append(value),
    )
    near_product = jnp.concatenate(near_product, axis=1)
    later = jnp.concatenate(later, axis=1)
    product_high, product_low = halves(stack(near_product, later[RANK:]))

    sized(arrived_first.at[pl.ds(0, 2 * SIDE - 1)], gram_send.at[0], gram_sem.at[0]).wait_recv()
    near_fold, far_fold = (
        (fold_got[h, 0] + fold_got[h, 1]) + (fold_got[h, 2] + fold_got[h, 3]) for h in range(2)
    )
    solved = eliminate(
        stack(
            jnp.where(narrow, near_fold, pltpu.roll(far_fold, 64, 1)),
            jnp.where(narrow, pltpu.roll(near_fold, 64, 1), far_fold),
        ),
        True,
    )
    near_inverse, far_inverse = solved[:, :32], solved[:, 64:96]
    mixing = 0.5 * stack(-solved[:, 32:64], solved[:, 96:128])
    mixing_high, mixing_low = halves(mixing)

    def mixed(high, low):
        return fast_dot(mixing_high, high, FIRST) + (
            fast_dot(mixing_high, low, FIRST) + fast_dot(mixing_low, high, FIRST)
        )

    terms = later[:RANK] + mixed(product_high, product_low)
    for part in range(4):
        put(1, terms[:, part * 256 : part * 256 + 256], part)
    send_over_rows(1)

    factor = late + mixed(stack(near_high, far_high), stack(near_low, far_low))
    factor_high, factor_low = halves(factor)
    nothing = jnp.zeros((RANK, WIDTH), jnp.bfloat16)
    block = fast_dot(
        stack(factor_high, factor_low),
        stack(
            factor_high, near_high, far_high, nothing,
            factor_low, near_low, far_low, nothing,
        ),
        LAST,
    )
    gram_start(block[:RANK, :128] + (block[:RANK, 128:] + block[RANK:, :128]))

    @pl.when(col_owner)
    def _():
        owned_over_rows(0)
        for k in range(ISLANDS):
            sums_out[k, 0] = summed[0, k] + summed[0, partner[0, k]]
        for k in range(ISLANDS):
            sums_out[k, 1] = sums_out[partner[1, k], 0]

        def give(index, carry):
            k = far_island(index)
            for near in range(2):
                m = (row + 3 + side + near) % SIDE
                pltpu.make_async_remote_copy(
                    sums_out.at[k], sums_in.at[row, island // 2], back_sem.at[2], get_sem.at[2],
                    device_id=device(k, m, other), device_id_type=MESH,
                ).start()
            return carry

        lax.fori_loop(0, ISLANDS, give, 0, unroll=True)


    left_ref[:RANK, :] = 0.5 * exact_dot(near_inverse, near, PLAIN)

    @pl.when(col_owner)
    def _():
        owned_over_rows(1)
        for k in range(ISLANDS):
            last_out[k, 0] = summed[1, k] + summed[1, partner[1, k]]
        give_over_rows(3, last_out, last_in)

    sized(arrived.at[0, pl.ds(0, TILES)], back_sem.at[2], get_sem.at[2]).wait_recv()
    passed = []
    for index, (source, target) in enumerate(
        (((row + side) % SIDE, (row + 3) % SIDE), ((row + side + 3) % SIDE, (row + 1) % SIDE))
    ):
        copy = pltpu.make_async_remote_copy(
            sums_in.at[source], sums_in.at[source], pass_send.at[index], pass_sem.at[index],
            device_id=device(island, target, col), device_id_type=MESH,
        )
        copy.start()
        passed.append(copy)

    def whole_sums(which):
        def tile(index):
            k = index // 2
            return sums_in[index % 2 * 2 + (k + core) % 2, k // 2, which]

        return stack(
            *(
                jnp.concatenate([tile(a * BLOCKS + b) for b in range(BLOCKS)], axis=1)
                for a in range(4)
            )
        )

    crossed = gram_finish()
    left_ref[RANK:, :] = 0.5 * exact_dot(eliminate(crossed, False)[:, :32], factor, PLAIN)
    near_change = -0.5 * exact_dot(crossed[:, 32:64], near_inverse, PLAIN)
    far_change = 0.5 * exact_dot(crossed[:, 64:96], far_inverse, PLAIN)
    for copy in passed:
        copy.wait_recv()
    near_sums = whole_sums(0)
    right_ref[:RANK, :] = near_sums
    change_high, change_low = halves(jnp.concatenate([near_change, far_change], axis=1))
    sums_high, sums_low = halves(stack(near_sums, whole_sums(1)))
    change = fast_dot(change_high, sums_high, PLAIN) + (
        fast_dot(change_high, sums_low, PLAIN) + fast_dot(change_low, sums_high, PLAIN)
    )
    sized(last_in, back_sem.at[3], get_sem.at[3]).wait_recv()
    right_ref[RANK:, :] = whole(last_in, 0) + change

    for copy in mate_copies + passed:
        copy.wait_send()
    sized(arrived_first.at[pl.ds(0, 2 * SIDE - 1)], gram_send.at[0], gram_sem.at[0]).wait_send()
    sized(gram_got.at[pl.ds(0, SIDE - 1)], gram_send.at[1], gram_sem.at[1]).wait_send()
    for flow in range(2):
        sized(sent.at[flow], send_sem.at[flow + 1], own_sem.at[flow + 1]).wait_send()

    @pl.when(row_owner)
    def _():
        sized(first.at[pl.ds(0, TILES - 1)], send_sem.at[0], own_sem.at[0]).wait_send()
        sized(arrived_first.at[pl.ds(0, PEERS - 1)], back_sem.at[0], get_sem.at[0]).wait_send()

        @pl.when(late_share)
        def _():
            sized(late_in.at[pl.ds(0, 2 * ISLANDS - 1)], back_sem.at[1], get_sem.at[1]).wait_send()

        @pl.when(jnp.logical_not(late_share))
        def _():
            sized(late_in, back_sem.at[1], get_sem.at[1]).wait_send()

    @pl.when(jnp.logical_not(row_owner))
    def _():
        sized(first, send_sem.at[0], own_sem.at[0]).wait_send()

    @pl.when(col_owner)
    def _():
        for flow in (2, 3):
            sized(arrived.at[0], back_sem.at[flow], get_sem.at[flow]).wait_send()


def update_kernel(weights_ref, left_ref, right_ref, out_ref, updated, sem):
    parts, rows = updated.shape[:2]
    high, low = halves(right_ref[...])
    right_stack = stack(high, low, high)
    copies = []
    for part in range(parts):
        block = pl.ds(part * rows, rows)
        high, low = halves(left_ref[:, block])
        updated[part] = weights_ref[block, :] - fast_dot(stack(high, high, low), right_stack, FIRST)
        copy = pltpu.make_async_copy(updated.at[part], out_ref.at[0, block, :], sem.at[part])
        copy.start()
        copies.append(copy)
    for copy in copies:
        copy.wait()


def shards(weights, bases, pairs):
    vmem = pl.BlockSpec(memory_space=pltpu.VMEM)
    hbm = pl.BlockSpec(memory_space=pltpu.HBM)
    factors = jax.ShapeDtypeStruct((2 * RANK, WIDTH), jnp.float32)
    tile = jax.ShapeDtypeStruct((WIDTH, WIDTH), jnp.float32)

    def tiles(*lead):
        return pltpu.VMEM((*lead, 8, 128), jnp.float32)

    dma = pltpu.SemaphoreType.DMA
    left, right, plain = pl.pallas_call(
        exchange_kernel,
        out_shape=(factors, factors, tile),
        in_specs=[hbm, hbm, pl.BlockSpec(memory_space=pltpu.SMEM)],
        out_specs=(vmem, vmem, vmem),
        scratch_shapes=[
            pltpu.VMEM((WIDTH, WIDTH), jnp.bfloat16),
            pltpu.VMEM((WIDTH, WIDTH), jnp.bfloat16),
            pltpu.VMEM((2, RANK, WIDTH), jnp.float32),
            pltpu.SMEM((2, ISLANDS), jnp.int32),
            tiles(TILES, 2), tiles(PEERS, 2),
            tiles(2, TILES), tiles(2, PEERS), tiles(2, ISLANDS),
            tiles(2, ISLANDS, 2), tiles(ISLANDS, 1), tiles(ISLANDS, 2), tiles(ISLANDS, 1),
            tiles(TILES, 2), tiles(TILES, 1), tiles(SIDE, TILES // SIDE, 2), tiles(TILES, 1),
            pltpu.VMEM((2, RANK, WIDTH), jnp.float32),
            pltpu.VMEM((RANK // 2, 128), jnp.float32),
            pltpu.VMEM((2, SIDE, RANK // 2, 128), jnp.float32),
            pltpu.VMEM((RANK, 128), jnp.float32),
            pltpu.VMEM((SIDE, RANK, 128), jnp.float32),
            dma((5,)), dma((3,)), dma((3,)), dma((4,)), dma((4,)), dma((2,)), dma((2,)), dma((2,)), dma((2,)), dma((2,)), dma((2,)),
        ],
        compiler_params=pltpu.CompilerParams(
            collective_id=0, has_side_effects=True, vmem_limit_bytes=32 * 2**20
        ),
        name="exchange",
    )(*(pltpu.with_memory_space_constraint(x, pltpu.HBM) for x in (weights, bases, pairs.transpose(0, 2, 1))))
    parts = 8
    return pl.pallas_call(
        update_kernel,
        out_shape=jax.ShapeDtypeStruct(weights.shape, jnp.float32),
        in_specs=[vmem, vmem, vmem],
        out_specs=hbm,
        scratch_shapes=[pltpu.VMEM((parts, WIDTH // parts, WIDTH), jnp.float32), dma((parts,))],
        compiler_params=pltpu.CompilerParams(vmem_limit_bytes=20 * 2**20),
        name="update",
    )(plain, left, right)


def solution(mesh):
    in_specs = (P("island", "row", "col"), P(None, None, "col"), P())
    out_specs = P("island", "row", "col")
    return jax.shard_map(shards, mesh=mesh, in_specs=in_specs, out_specs=out_specs, check_vma=False)
```

```python
import jax
import jax.numpy as jnp
from jax import lax
from jax.experimental import pallas as pl
from jax.experimental.pallas import tpu as pltpu
from jax.sharding import PartitionSpec as P

MESH = pl.DeviceIdType.MESH
RANK = 32
WIDTH = 1024
TILES = 32
BLOCKS = WIDTH // 128
ISLANDS = 16
SIDE = 4
PEERS = ISLANDS * SIDE
BLOCK = 8
HIGHEST = lax.Precision.HIGHEST
LAST = (((1,), (1,)), ((), ()))
FIRST = (((0,), (0,)), ((), ()))
PLAIN = (((1,), (0,)), ((), ()))


def halves(array):
    high = array.astype(jnp.bfloat16)
    low = (array - high.astype(jnp.float32)).astype(jnp.bfloat16)
    return high, low


def device(island, row, col):
    return {"island": island, "row": row, "col": col}


def exact_dot(left, right, dims):
    return lax.dot_general(left, right, dims, precision=HIGHEST, preferred_element_type=jnp.float32)


def fast_dot(left, right, dims):
    return lax.dot_general(left, right, dims, preferred_element_type=jnp.float32)


def stack(*rows):
    return jnp.concatenate(rows, axis=0)


def eliminate(matrix, double):
    rows = lax.broadcasted_iota(jnp.int32, (RANK, 128), 0)
    lanes = lax.broadcasted_iota(jnp.int32, (1, 128), 1)
    position = lanes % 64 if double else lanes
    for start in range(0, RANK, BLOCK):
        pivots = range(start, start + BLOCK)
        factors = []
        for pivot in pivots:
            factor = jnp.broadcast_to(matrix[:, pivot : pivot + 1], (RANK, 128))
            if double:
                second = jnp.broadcast_to(matrix[:, 64 + pivot : 65 + pivot], (RANK, 128))
                factor = jnp.where(lanes < 64, factor, second)
            factors.append(factor)
        here = (position >= start) & (position < start + BLOCK)
        solved = [
            jnp.where(here, jnp.where(position == pivot, 1.0, 0.0), matrix[pivot : pivot + 1])
            for pivot in pivots
        ]
        corner = [[factor[pivot : pivot + 1] for factor in factors] for pivot in pivots]
        for j in range(BLOCK):
            scale = 1.0 / corner[j][j]
            solved[j] = solved[j] * scale
            corner[j] = [entry * scale if m > j else entry for m, entry in enumerate(corner[j])]
            for i in range(j + 1, BLOCK):
                solved[i] = solved[i] - corner[i][j] * solved[j]
                corner[i] = [
                    entry - corner[i][j] * corner[j][m] if m > j else entry
                    for m, entry in enumerate(corner[i])
                ]
        for j in reversed(range(BLOCK)):
            for i in range(j):
                solved[i] = solved[i] - corner[i][j] * solved[j]
        rest = jnp.where(here, 0.0, matrix)
        for factor, row in zip(factors, solved):
            rest = rest - factor * row
        for pivot, row in zip(pivots, solved):
            rest = jnp.where(rows == pivot, row, rest)
        matrix = rest
    return matrix


def exchange_kernel(
    weights_ref, bases_ref, pairs_ref, left_ref, right_ref, plain,
    high_ref, low_ref, bases_in, partner, first, arrived_first, sent, arrived, summed,
    pair_out, late_out, sums_out, last_out, pair_in, late_in, sums_in, last_in,
    factors_in, fold_sent, fold_got, gram_sent, gram_got,
    load_sem, send_sem, own_sem, back_sem, get_sem, mate_send, mate_sem, pass_send, pass_sem, gram_send, gram_sem,
):
    island, row, col = (lax.axis_index(name) for name in ("island", "row", "col"))
    side, core = col // 2, col % 2
    other = (1 - side) * 2 + core
    mate = side * 2 + 1 - core

    base_load = pltpu.make_async_copy(bases_ref, bases_in, load_sem.at[4])
    base_load.start()
    loads = []
    for part in range(4):
        rows = pl.ds(part * 256, 256)
        load = pltpu.make_async_copy(
            weights_ref.at[0, rows, :], plain.at[rows, :], load_sem.at[part]
        )
        load.start()
        loads.append(load)

    barrier = pltpu.get_barrier_semaphore()
    across, along = island // SIDE, island % SIDE

    def far_first(index):
        return (2 + 3 * index + 3 * (index * (index - 1) // 2)) % SIDE

    def far_island(index):
        return (across + far_first(index // SIDE)) % SIDE * SIDE + (along + far_first(index % SIDE)) % SIDE

    for step in range(1, SIDE):
        pl.semaphore_signal(
            barrier, inc=1, device_id=device(island, (row + step) % SIDE, col), device_id_type=MESH
        )

    row_owner = core == island % 2

    @pl.when(row_owner)
    def _():
        def greet(index, carry):
            k = far_island(index)
            for m in range(SIDE):

                @pl.when((k != island) | (m != col))
                def _():
                    pl.semaphore_signal(barrier, inc=1, device_id=device(k, row, m), device_id_type=MESH)

            return carry

        lax.fori_loop(0, ISLANDS, greet, 0, unroll=True)

    base_load.wait()
    base_high, base_low = halves(bases_in[...].reshape(2 * RANK, WIDTH))
    base_stack = stack(base_high, base_low)

    def put_first(value, part):
        for basis in range(2):
            for a in range(4):
                for b in range(2):
                    first[a * BLOCKS + part * 2 + b, basis] = value[
                        basis * RANK + a * 8 : basis * RANK + a * 8 + 8, b * 128 : b * 128 + 128
                    ]

    def put(flow, value, part):
        for a in range(4):
            for b in range(2):
                sent[flow, a * BLOCKS + part * 2 + b] = value[a * 8 : a * 8 + 8, b * 128 : b * 128 + 128]

    for part in range(4):
        loads[part].wait()
        rows = pl.ds(part * 256, 256)
        high, low = halves(plain[rows, :])
        high_ref[rows, :] = high
        low_ref[rows, :] = low
        wide = fast_dot(base_stack, high, LAST)
        fine = fast_dot(base_high, low, LAST)
        terms = wide[: 2 * RANK] + (wide[2 * RANK :] + fine)
        put_first(terms, part)

    pl.semaphore_wait(barrier, TILES - row_owner.astype(jnp.int32) + SIDE - 1)

    row_tile = island * 2 + side
    col_owner = row % 2 == (island + core) % 2
    col_tile = island * 2 + row // 2

    def sized(ref, send, recv):
        return pltpu.make_async_remote_copy(
            ref, ref, send, recv, device_id=device(island, row, other), device_id_type=MESH
        )

    def add_up(flow):
        for k in range(ISLANDS):
            summed[flow, k] = (arrived[flow, k * 4] + arrived[flow, k * 4 + 1]) + (
                arrived[flow, k * 4 + 2] + arrived[flow, k * 4 + 3]
            )

    def send_over_columns():
        def send(index, carry):
            k = far_island(index)
            for which in range(2):
                m = which * 2 + k % 2

                @pl.when((k != island) | (m != col))
                def _():
                    pltpu.make_async_remote_copy(
                        first.at[2 * k + which], arrived_first.at[island * 4 + col],
                        send_sem.at[0], own_sem.at[0],
                        device_id=device(k, row, m), device_id_type=MESH,
                    ).start()

            return carry

        lax.fori_loop(0, ISLANDS, send, 0, unroll=True)

    def give_pairs():
        def give(index, carry):
            k = far_island(index)
            for m in range(SIDE):

                @pl.when((k != island) | (m != col))
                def _():
                    pltpu.make_async_remote_copy(
                        pair_out.at[m % 2, k], pair_in.at[row_tile], back_sem.at[0], get_sem.at[0],
                        device_id=device(k, row, m), device_id_type=MESH,
                    ).start()

            return carry

        lax.fori_loop(0, ISLANDS, give, 0, unroll=True)
        pair_in[row_tile] = pair_out[core, island]

    def give_late():
        def give(index, carry):
            k = far_island(index)
            for half in range(2):
                m = half * 2 + row_tile // 16

                @pl.when((k != island) | (m != col))
                def _():
                    pltpu.make_async_remote_copy(
                        late_out.at[k], late_in.at[row_tile], back_sem.at[1], get_sem.at[1],
                        device_id=device(k, row, m), device_id_type=MESH,
                    ).start()

            return carry

        lax.fori_loop(0, ISLANDS, give, 0, unroll=True)

        @pl.when(row_tile // 16 == core)
        def _():
            late_in[row_tile] = late_out[island]

    def send_over_rows(flow):
        def send(index, carry):
            k = far_island(index)
            for which in range(2):
                pltpu.make_async_remote_copy(
                    sent.at[flow, 2 * k + which], arrived.at[flow, island * 4 + row],
                    send_sem.at[flow + 1], own_sem.at[flow + 1],
                    device_id=device(k, which * 2 + (k + core) % 2, other), device_id_type=MESH,
                ).start()
            return carry

        lax.fori_loop(0, ISLANDS, send, 0, unroll=True)

    def owned_over_rows(flow):
        sized(arrived.at[flow], send_sem.at[flow + 1], own_sem.at[flow + 1]).wait_recv()
        add_up(flow)

    def give_over_rows(flow, out, into):
        def give(index, carry):
            k = far_island(index)
            for near in range(SIDE):
                m = (row + 1 + side + near) % SIDE
                pltpu.make_async_remote_copy(
                    out.at[k], into.at[col_tile], back_sem.at[flow], get_sem.at[flow],
                    device_id=device(k, m, other), device_id_type=MESH,
                ).start()
            return carry

        lax.fori_loop(0, ISLANDS, give, 0, unroll=True)

    def whole(ref, which):
        return stack(
            *(
                jnp.concatenate([ref[a * BLOCKS + b, which] for b in range(BLOCKS)], axis=1)
                for a in range(4)
            )
        )

    def to_mate(source, target, index):
        copy = pltpu.make_async_remote_copy(
            source, target, mate_send.at[index], mate_sem.at[index],
            device_id=device(island, row, mate), device_id_type=MESH,
        )
        copy.start()
        return copy

    def gram_start(gram):
        gram_sent[...] = gram
        gram_got[row] = gram
        for step in range(1, SIDE):
            pltpu.make_async_remote_copy(
                gram_sent, gram_got.at[row], gram_send.at[1], gram_sem.at[1],
                device_id=device(island, (row + step) % SIDE, col), device_id_type=MESH,
            ).start()

    def gram_finish():
        sized(gram_got.at[pl.ds(0, SIDE - 1)], gram_send.at[1], gram_sem.at[1]).wait_recv()
        return (gram_got[0] + gram_got[1]) + (gram_got[2] + gram_got[3])

    def times_weights(high, low, count, use):
        both = stack(high, low)
        for part in range(4):
            cols = pl.ds(part * 256, 256)
            wide = fast_dot(both, high_ref[:, cols], PLAIN)
            fine = fast_dot(high, low_ref[:, cols], PLAIN)
            use(wide[:count] + (wide[count:] + fine), part)

    send_over_columns()

    def find(index, carry):
        for matching in range(2):
            found = jnp.int32(0)
            for pair in range(ISLANDS // 2):
                first, second = pairs_ref[matching, 0, pair], pairs_ref[matching, 1, pair]
                found += jnp.where(first == index, second, 0) + jnp.where(second == index, first, 0)
            partner[matching, index] = found
        return carry

    lax.fori_loop(0, ISLANDS, find, 0)

    @pl.when(row_owner)
    def _():
        arrived_first[island * 4 + col] = first[row_tile]
        sized(arrived_first.at[pl.ds(0, PEERS - 1)], send_sem.at[0], own_sem.at[0]).wait_recv()
        for k in range(ISLANDS):
            for basis in range(2):
                summed[basis, k] = (
                    arrived_first[k * 4, basis] + arrived_first[k * 4 + 1, basis]
                ) + (arrived_first[k * 4 + 2, basis] + arrived_first[k * 4 + 3, basis])
        for k in range(ISLANDS):
            for basis in range(2):
                pair_out[0, k, basis] = summed[basis, k] - summed[basis, partner[0, k]]
        for k in range(ISLANDS):
            pair_out[1, k] = pair_out[0, partner[1, k]]
        give_pairs()
        for k in range(ISLANDS):
            late_out[k, 0] = summed[1, k] - summed[1, partner[1, k]]
        give_late()
        sized(pair_in.at[pl.ds(0, TILES - 1)], back_sem.at[0], get_sem.at[0]).wait_recv()

    @pl.when(jnp.logical_not(row_owner))
    def _():
        sized(pair_in, back_sem.at[0], get_sem.at[0]).wait_recv()

    mine = whole(pair_in, 0)
    factors_in[core] = mine
    mate_copies = [to_mate(factors_in.at[core], factors_in.at[core], 0)]
    mine_high, mine_low = halves(mine)
    cross_high, cross_low = halves(whole(pair_in, 1))
    block = fast_dot(
        stack(mine_high, mine_low),
        stack(mine_high, cross_high, mine_high, cross_high, mine_low, cross_low, mine_low, cross_low),
        LAST,
    )
    block = block[:RANK, :128] + (block[:RANK, 128:] + block[RANK:, :128])
    narrow = lax.broadcasted_iota(jnp.int32, (RANK // 2, 128), 1) < 64
    fold_sent[...] = jnp.where(narrow, block[: RANK // 2], block[RANK // 2 :])
    fold_got[core, row] = fold_sent[...]

    def fold(index, carry):
        m, h = (row + 1 + index // 2) % SIDE, index % 2

        @pl.when((m != row) | (h != core))
        def _():
            pltpu.make_async_remote_copy(
                fold_sent, fold_got.at[core, row], gram_send.at[0], gram_sem.at[0],
                device_id=device(island, m, side * 2 + h), device_id_type=MESH,
            ).start()

        return carry

    lax.fori_loop(0, 2 * SIDE, fold, 0)

    late_share = row_owner & (row_tile // 16 == core)

    @pl.when(late_share)
    def _():
        sized(late_in.at[pl.ds(0, TILES // 2 - 1)], back_sem.at[1], get_sem.at[1]).wait_recv()

    @pl.when(jnp.logical_not(late_share))
    def _():
        sized(late_in.at[pl.ds(0, TILES // 2)], back_sem.at[1], get_sem.at[1]).wait_recv()

    share = late_in.at[pl.ds(core * 16, 16)]
    mate_copies.append(to_mate(share, share, 1))
    mate_copies[0].wait_recv()
    near, far = factors_in[0], factors_in[1]
    near_high, near_low = halves(near)
    far_high, far_low = halves(far)
    near_product, later = [], []

    def use_near(value, part):
        put(0, value, part)
        near_product.append(value)

    times_weights(near_high, near_low, RANK, use_near)
    send_over_rows(0)
    mate_copies[1].wait_recv()
    late = whole(late_in, 0)
    late_high, late_low = halves(late)
    times_weights(
        stack(late_high, far_high), stack(late_low, far_low), 2 * RANK,
        lambda value, part: later.append(value),
    )
    near_product = jnp.concatenate(near_product, axis=1)
    later = jnp.concatenate(later, axis=1)
    product_high, product_low = halves(stack(near_product, later[RANK:]))

    sized(arrived_first.at[pl.ds(0, 2 * SIDE - 1)], gram_send.at[0], gram_sem.at[0]).wait_recv()
    near_fold, far_fold = (
        (fold_got[h, 0] + fold_got[h, 1]) + (fold_got[h, 2] + fold_got[h, 3]) for h in range(2)
    )
    solved = eliminate(
        stack(
            jnp.where(narrow, near_fold, pltpu.roll(far_fold, 64, 1)),
            jnp.where(narrow, pltpu.roll(near_fold, 64, 1), far_fold),
        ),
        True,
    )
    near_inverse, far_inverse = solved[:, :32], solved[:, 64:96]
    mixing = 0.5 * stack(-solved[:, 32:64], solved[:, 96:128])
    mixing_high, mixing_low = halves(mixing)
    mixing_stack = stack(mixing_high, mixing_high, mixing_low)

    def mixed(high, low):
        return fast_dot(mixing_stack, stack(high, low, high), FIRST)

    terms = later[:RANK] + mixed(product_high, product_low)
    for part in range(4):
        put(1, terms[:, part * 256 : part * 256 + 256], part)
    send_over_rows(1)

    @pl.when(col_owner)
    def _():
        owned_over_rows(0)
        for k in range(ISLANDS):
            sums_out[k, 0] = summed[0, k] + summed[0, partner[0, k]]
        for k in range(ISLANDS):
            sums_out[k, 1] = sums_out[partner[1, k], 0]

        def give(index, carry):
            k = far_island(index)
            for near in range(2):
                m = (row + 3 + side + near) % SIDE
                pltpu.make_async_remote_copy(
                    sums_out.at[k], sums_in.at[row, island // 2], back_sem.at[2], get_sem.at[2],
                    device_id=device(k, m, other), device_id_type=MESH,
                ).start()
            return carry

        lax.fori_loop(0, ISLANDS, give, 0, unroll=True)


    factor = late + mixed(stack(near_high, far_high), stack(near_low, far_low))
    factor_high, factor_low = halves(factor)
    nothing = jnp.zeros((RANK, WIDTH), jnp.bfloat16)
    block = fast_dot(
        stack(factor_high, factor_low),
        stack(
            factor_high, near_high, far_high, nothing,
            factor_low, near_low, far_low, nothing,
        ),
        LAST,
    )
    gram_start(block[:RANK, :128] + (block[:RANK, 128:] + block[RANK:, :128]))

    left_ref[:RANK, :] = 0.5 * exact_dot(near_inverse, near, PLAIN)

    @pl.when(col_owner)
    def _():
        owned_over_rows(1)
        for k in range(ISLANDS):
            last_out[k, 0] = summed[1, k] + summed[1, partner[1, k]]
        give_over_rows(3, last_out, last_in)

    sized(arrived.at[0, pl.ds(0, TILES)], back_sem.at[2], get_sem.at[2]).wait_recv()
    passed = []
    for index, (source, target) in enumerate(
        (((row + side) % SIDE, (row + 3) % SIDE), ((row + side + 3) % SIDE, (row + 1) % SIDE))
    ):
        copy = pltpu.make_async_remote_copy(
            sums_in.at[source], sums_in.at[source], pass_send.at[index], pass_sem.at[index],
            device_id=device(island, target, col), device_id_type=MESH,
        )
        copy.start()
        passed.append(copy)

    def whole_sums(which):
        def tile(index):
            k = index // 2
            return sums_in[index % 2 * 2 + (k + core) % 2, k // 2, which]

        return stack(
            *(
                jnp.concatenate([tile(a * BLOCKS + b) for b in range(BLOCKS)], axis=1)
                for a in range(4)
            )
        )

    crossed = gram_finish()
    left_ref[RANK:, :] = 0.5 * exact_dot(eliminate(crossed, False)[:, :32], factor, PLAIN)
    near_change = -0.5 * exact_dot(crossed[:, 32:64], near_inverse, PLAIN)
    far_change = 0.5 * exact_dot(crossed[:, 64:96], far_inverse, PLAIN)
    for copy in passed:
        copy.wait_recv()
    near_sums = whole_sums(0)
    right_ref[:RANK, :] = near_sums
    change_high, change_low = halves(jnp.concatenate([near_change, far_change], axis=1))
    sums_high, sums_low = halves(stack(near_sums, whole_sums(1)))
    change = fast_dot(change_high, sums_high, PLAIN) + (
        fast_dot(change_high, sums_low, PLAIN) + fast_dot(change_low, sums_high, PLAIN)
    )
    sized(last_in, back_sem.at[3], get_sem.at[3]).wait_recv()
    right_ref[RANK:, :] = whole(last_in, 0) + change

    for copy in mate_copies + passed:
        copy.wait_send()
    sized(arrived_first.at[pl.ds(0, 2 * SIDE - 1)], gram_send.at[0], gram_sem.at[0]).wait_send()
    sized(gram_got.at[pl.ds(0, SIDE - 1)], gram_send.at[1], gram_sem.at[1]).wait_send()
    for flow in range(2):
        sized(sent.at[flow], send_sem.at[flow + 1], own_sem.at[flow + 1]).wait_send()

    @pl.when(row_owner)
    def _():
        sized(first.at[pl.ds(0, TILES - 1)], send_sem.at[0], own_sem.at[0]).wait_send()
        sized(arrived_first.at[pl.ds(0, PEERS - 1)], back_sem.at[0], get_sem.at[0]).wait_send()

        @pl.when(late_share)
        def _():
            sized(late_in.at[pl.ds(0, 2 * ISLANDS - 1)], back_sem.at[1], get_sem.at[1]).wait_send()

        @pl.when(jnp.logical_not(late_share))
        def _():
            sized(late_in, back_sem.at[1], get_sem.at[1]).wait_send()

    @pl.when(jnp.logical_not(row_owner))
    def _():
        sized(first, send_sem.at[0], own_sem.at[0]).wait_send()

    @pl.when(col_owner)
    def _():
        for flow in (2, 3):
            sized(arrived.at[0], back_sem.at[flow], get_sem.at[flow]).wait_send()


def update_kernel(weights_ref, left_ref, right_ref, out_ref, updated, sem):
    parts, rows = updated.shape[:2]
    high, low = halves(right_ref[...])
    right_stack = stack(high, low, high)
    copies = []
    for part in range(parts):
        block = pl.ds(part * rows, rows)
        high, low = halves(left_ref[:, block])
        updated[part] = weights_ref[block, :] - fast_dot(stack(high, high, low), right_stack, FIRST)
        copy = pltpu.make_async_copy(updated.at[part], out_ref.at[0, block, :], sem.at[part])
        copy.start()
        copies.append(copy)
    for copy in copies:
        copy.wait()


def shards(weights, bases, pairs):
    vmem = pl.BlockSpec(memory_space=pltpu.VMEM)
    hbm = pl.BlockSpec(memory_space=pltpu.HBM)
    factors = jax.ShapeDtypeStruct((2 * RANK, WIDTH), jnp.float32)
    tile = jax.ShapeDtypeStruct((WIDTH, WIDTH), jnp.float32)

    def tiles(*lead):
        return pltpu.VMEM((*lead, 8, 128), jnp.float32)

    dma = pltpu.SemaphoreType.DMA
    left, right, plain = pl.pallas_call(
        exchange_kernel,
        out_shape=(factors, factors, tile),
        in_specs=[hbm, hbm, pl.BlockSpec(memory_space=pltpu.SMEM)],
        out_specs=(vmem, vmem, vmem),
        scratch_shapes=[
            pltpu.VMEM((WIDTH, WIDTH), jnp.bfloat16),
            pltpu.VMEM((WIDTH, WIDTH), jnp.bfloat16),
            pltpu.VMEM((2, RANK, WIDTH), jnp.float32),
            pltpu.SMEM((2, ISLANDS), jnp.int32),
            tiles(TILES, 2), tiles(PEERS, 2),
            tiles(2, TILES), tiles(2, PEERS), tiles(2, ISLANDS),
            tiles(2, ISLANDS, 2), tiles(ISLANDS, 1), tiles(ISLANDS, 2), tiles(ISLANDS, 1),
            tiles(TILES, 2), tiles(TILES, 1), tiles(SIDE, TILES // SIDE, 2), tiles(TILES, 1),
            pltpu.VMEM((2, RANK, WIDTH), jnp.float32),
            pltpu.VMEM((RANK // 2, 128), jnp.float32),
            pltpu.VMEM((2, SIDE, RANK // 2, 128), jnp.float32),
            pltpu.VMEM((RANK, 128), jnp.float32),
            pltpu.VMEM((SIDE, RANK, 128), jnp.float32),
            dma((5,)), dma((3,)), dma((3,)), dma((4,)), dma((4,)), dma((2,)), dma((2,)), dma((2,)), dma((2,)), dma((2,)), dma((2,)),
        ],
        compiler_params=pltpu.CompilerParams(
            collective_id=0, has_side_effects=True, vmem_limit_bytes=32 * 2**20
        ),
        name="exchange",
    )(*(pltpu.with_memory_space_constraint(x, pltpu.HBM) for x in (weights, bases, pairs.transpose(0, 2, 1))))
    parts = 8
    return pl.pallas_call(
        update_kernel,
        out_shape=jax.ShapeDtypeStruct(weights.shape, jnp.float32),
        in_specs=[vmem, vmem, vmem],
        out_specs=hbm,
        scratch_shapes=[pltpu.VMEM((parts, WIDTH // parts, WIDTH), jnp.float32), dma((parts,))],
        compiler_params=pltpu.CompilerParams(vmem_limit_bytes=20 * 2**20),
        name="update",
    )(plain, left, right)


def solution(mesh):
    in_specs = (P("island", "row", "col"), P(None, None, "col"), P())
    out_specs = P("island", "row", "col")
    return jax.shard_map(shards, mesh=mesh, in_specs=in_specs, out_specs=out_specs, check_vma=False)
```
